32 devices in a mesh: seq: 2 (over core), ctx: 8 (over z, x), wt: 2 (over y).
Axes of the slice: x: 2, y: 2, z: 4, core: 2. Of those that a mesh axis runs over, the one named last changes fastest.
Arguments:
- layer_input: bfloat16 [2, 1024, 576], P('seq', 'ctx', 'wt'), may hold values from -32 to 32
- cotangent: bfloat16 [2, 1024, 576], P('seq', 'ctx', 'wt'), may hold values from -6 to 6
- w_qkv: bfloat16 [576, 960], P('wt'), may hold values from -0.25 to 0.25
- w_out: bfloat16 [576, 576], P(None, 'wt'), may hold values from -1.5 to 1.5
- w_gate: bfloat16 [576, 1536], P(None, 'wt'), may hold values from -0.25 to 0.25
- w_up: bfloat16 [576, 1536], P(None, 'wt'), may hold values from -0.25 to 0.25
- w_down: bfloat16 [1536, 576], P('wt'), may hold values from -0.3125 to 0.3125
- gain_attn: float32 [576], P('wt'), may hold values from 0.1 to 1.9
- gain_mlp: float32 [576], P('wt'), may hold values from 0.1 to 1.9
Outputs:
- layer_output: bfloat16 [2, 1024, 576], P('seq', 'ctx', 'wt')
- input_grad: float32 [2, 1024, 576], P('seq', 'ctx', 'wt')
- grad_qkv: float32 [576, 960], P('wt')
- grad_out: float32 [576, 576], P(None, 'wt')
- grad_gate: float32 [576, 1536], P(None, 'wt')
- grad_up: float32 [576, 1536], P(None, 'wt')
- grad_down: float32 [1536, 576], P('wt')
- grad_gain_attn: float32 [576], P('wt')
- grad_gain_mlp: float32 [576], P('wt')
The draws below stay inside these ranges and needn't reach their ends.
All inputs are finite; a program needn't handle non-finite values.
Results may differ from the reference program's by a relative error of at most 0.04.
Values may be sent and summed in bfloat16 or wider, within the bound.
No kernel may reach another device: no remote copies, remote signals or barrier semaphores. Data moves between devices by JAX's collectives and lax.ppermute only.
A program may use at most 128 MiB of HBM per device.

```python
import jax
import jax.numpy as jnp
from jax import lax

D = 576
QUERY_HEADS = 9
KEY_VALUE_HEADS = 3
HEAD_SIZE = 64
FF = 1536
TOK_DEV = 128
SEQS = 2
SEQUENCE_TOKENS = 1024
BLOCK = 64
PIECE = 32
NBLOCKS = 16


def draw_layer_input(key, part):
    normal_key = jax.random.fold_in(key, 11)
    column = jnp.exp(jnp.log(3.0) * jnp.arange(D, dtype=jnp.float32) / (D - 1))
    gauss_draw = jax.random.normal(normal_key, (SEQS, SEQUENCE_TOKENS, D), jnp.float32)
    values = gauss_draw * column
    return jnp.clip(values, -32.0, 32.0).astype(jnp.bfloat16)


def draw_w_qkv(key, part):
    query_key_value_width = (QUERY_HEADS + 2 * KEY_VALUE_HEADS) * HEAD_SIZE
    spread = jnp.sqrt(2.0 / D)
    values = jax.random.normal(jax.random.fold_in(key, 21), (D, query_key_value_width), jnp.float32) * spread
    return jnp.clip(values, -0.25, 0.25).astype(jnp.bfloat16)


def block_levels(stream_key, dims, shards, smallest, high):
    factor_of, own = 1.0, jax.random.fold_in(stream_key, 6)
    for axis_at, parts in shards:
        steps = jnp.exp(jax.random.uniform(jax.random.fold_in(own, axis_at), (parts,), jnp.float32, smallest / len(shards), high / len(shards)))
        factor_of = factor_of * jnp.repeat(steps, dims[axis_at] // parts).reshape([-1 if axis == axis_at else 1 for axis in range(len(dims))])
    return factor_of


def noise(rng, extent, scale, most, cuts=(), held_as=jnp.bfloat16):
    level = block_levels(rng, extent, cuts, -0.22, 0.18) if cuts else 1.0
    values = jax.random.normal(rng, extent, jnp.float32) * scale * level
    return jnp.minimum(jnp.maximum(values, -most), most).astype(held_as)


def setup_inputs(seed: int = 0) -> dict:
    key_of = jax.random.split(jax.random.key(seed), 10)
    return {
        "layer_input": draw_layer_input(jax.random.fold_in(key_of[9], 71), 0),
        "cotangent": noise(key_of[1], (SEQS, SEQUENCE_TOKENS, D), 1.0, 6.0, ((0, 2), (1, 8), (2, 2))),
        "w_qkv": draw_w_qkv(jax.random.fold_in(key_of[9], 71), 0),
        "w_out": noise(key_of[3], (QUERY_HEADS * HEAD_SIZE, D), (HEAD_SIZE // 4) ** -0.5, 1.5, ((1, 2),)),
        "w_gate": noise(key_of[4], (D, FF), D ** -0.5, 0.25, ((1, 2),)),
        "w_up": noise(key_of[5], (D, FF), D ** -0.5, 0.25, ((1, 2),)),
        "w_down": noise(key_of[6], (FF, D), (FF // 4) ** -0.5, 0.3125, ((0, 2),)),
        "gain_attn": jnp.clip(1.0 + 0.18 * jax.random.normal(key_of[7], (D,), jnp.float32), 0.1, 1.9),
        "gain_mlp": jnp.clip(1.0 + 0.18 * jax.random.normal(key_of[8], (D,), jnp.float32), 0.1, 1.9),
    }


EPSILON = 1e-05
ROPE_BASE = 100000.0

def rounded_values(tensor):
    return lax.optimization_barrier(tensor.astype(jnp.bfloat16))

def dealt_positions():
    row_index = jnp.arange(SEQUENCE_TOKENS, dtype=jnp.int32)
    owner_ctx = row_index // TOK_DEV
    within = row_index % TOK_DEV
    slot_index = within // PIECE
    block_id = jnp.where(slot_index % 2 == 1, NBLOCKS - 1 - owner_ctx, owner_ctx)
    return block_id * BLOCK + slot_index // 2 * PIECE + within % PIECE

def rope_tables(positions):
    half_dim = HEAD_SIZE // 2
    frequency = jnp.power(jnp.float32(ROPE_BASE), -jnp.arange(half_dim, dtype=jnp.float32) * 2.0 / HEAD_SIZE)
    angles = positions.astype(jnp.float32)[:, None] * frequency[None, :]
    angles = jnp.concatenate([angles, angles], axis=1)
    return (jnp.cos(angles), jnp.sin(angles))

def rotate(tensor):
    half_dim = tensor.shape[-1] // 2
    return jnp.concatenate([-tensor[..., half_dim:], tensor[..., :half_dim]], axis=-1)

def block_scores(query_block, key_float, row_start, block_length, key_pos):
    query_pos = row_start + jnp.arange(block_length, dtype=jnp.int32)
    scores = jnp.einsum('pgrd,kgd->pgrk', query_block.astype(jnp.float32), key_float) * 0.125
    key_mask = (key_pos[None, :] <= query_pos[:, None])[:, None, None, :]
    return (jnp.where(key_mask, scores, -1e+30), key_mask)

def attention_forward(query_rows, key_row_slice, value_row_slice):
    block_length = min(512, SEQUENCE_TOKENS)
    block_total = SEQUENCE_TOKENS // block_length
    repeat_factor = QUERY_HEADS // KEY_VALUE_HEADS
    key_float = key_row_slice.astype(jnp.float32)
    value_float = value_row_slice.astype(jnp.float32)
    key_pos = jnp.arange(SEQUENCE_TOKENS, dtype=jnp.int32)
    query_block_list = query_rows.reshape(block_total, block_length, KEY_VALUE_HEADS, repeat_factor, HEAD_SIZE)
    start_offsets = jnp.arange(block_total, dtype=jnp.int32) * block_length

    def single_block(block_pair):
        query_block, row_start = block_pair
        scores, key_mask = block_scores(query_block, key_float, row_start, block_length, key_pos)
        running_max = lax.optimization_barrier(jnp.max(scores, axis=-1, keepdims=True))
        summed_exp = lax.optimization_barrier(jnp.sum(jnp.where(key_mask, jnp.exp(scores - running_max), 0.0), axis=-1, keepdims=True))
        lse_block = running_max + jnp.log(summed_exp)
        attn_weight = rounded_values(jnp.where(key_mask, jnp.exp(scores - lse_block), 0.0))
        attended_rows = jnp.einsum('pgrk,kgd->pgrd', attn_weight.astype(jnp.float32), value_float)
        return (attended_rows.astype(jnp.bfloat16), lse_block[..., 0])
    attended_rows, logsumexp_every = lax.map(single_block, (query_block_list, start_offsets))
    return (attended_rows.reshape(SEQUENCE_TOKENS, KEY_VALUE_HEADS, repeat_factor, HEAD_SIZE), logsumexp_every.reshape(SEQUENCE_TOKENS, KEY_VALUE_HEADS, repeat_factor))

def attention_backward(query_rows, key_row_slice, value_row_slice, attended_rows, attended_gradient, logsumexp_every):
    block_length = min(512, SEQUENCE_TOKENS)
    block_total = SEQUENCE_TOKENS // block_length
    repeat_factor = QUERY_HEADS // KEY_VALUE_HEADS
    key_float = key_row_slice.astype(jnp.float32)
    value_float = value_row_slice.astype(jnp.float32)
    key_pos = jnp.arange(SEQUENCE_TOKENS, dtype=jnp.int32)
    start_offsets = jnp.arange(block_total, dtype=jnp.int32) * block_length
    reshaped_tensor = (block_total, block_length, KEY_VALUE_HEADS, repeat_factor, HEAD_SIZE)

    def single_block(loop_state, block_in):
        key_acc, value_acc = loop_state
        query_block, grad_block, out_block, lse_block, row_start = block_in
        scores, key_mask = block_scores(query_block, key_float, row_start, block_length, key_pos)
        probs_full = jnp.where(key_mask, jnp.exp(scores - lse_block[..., None]), 0.0)
        grad_float = grad_block.astype(jnp.float32)
        row_delta = lax.optimization_barrier(jnp.sum(grad_float * out_block.astype(jnp.float32), axis=-1))
        prob_grad = jnp.einsum('pgrd,kgd->pgrk', grad_float, value_float)
        score_grad = rounded_values(probs_full * (prob_grad - row_delta[..., None])).astype(jnp.float32)
        weight_bf = rounded_values(probs_full).astype(jnp.float32)
        query_gradient = jnp.einsum('pgrk,kgd->pgrd', score_grad, key_float) * 0.125
        key_acc = key_acc + jnp.einsum('pgrk,pgrd->kgd', score_grad, query_block.astype(jnp.float32)) * 0.125
        value_acc = value_acc + jnp.einsum('pgrk,pgrd->kgd', weight_bf, grad_float)
        return ((key_acc, value_acc), query_gradient)
    empty_rows = jnp.zeros((SEQUENCE_TOKENS, KEY_VALUE_HEADS, HEAD_SIZE), jnp.float32)
    (key_gradient, value_gradient), query_gradient = lax.scan(single_block, (empty_rows, empty_rows), (query_rows.reshape(reshaped_tensor), attended_gradient.reshape(reshaped_tensor), attended_rows.reshape(reshaped_tensor), logsumexp_every.reshape(block_total, block_length, KEY_VALUE_HEADS, repeat_factor), start_offsets))
    return (query_gradient.reshape(SEQUENCE_TOKENS, QUERY_HEADS, HEAD_SIZE), key_gradient, value_gradient)

def one_sequence(layer_rows, cot_rows, w_qkv, w_out, w_gate, w_up, w_down, gain_attn, gain_mlp):
    positions = dealt_positions()
    query_total_width = QUERY_HEADS * HEAD_SIZE
    key_value_width = KEY_VALUE_HEADS * HEAD_SIZE
    repeat_factor = QUERY_HEADS // KEY_VALUE_HEADS

    def natural(tensor):
        return jnp.zeros_like(tensor).at[positions].set(tensor)
    resid_in = layer_rows.astype(jnp.float32)
    scale_one = lax.rsqrt(lax.optimization_barrier(jnp.mean(resid_in * resid_in, axis=-1, keepdims=True)) + EPSILON)
    normed_one = resid_in * scale_one
    hidden_one = (normed_one * gain_attn).astype(jnp.bfloat16)
    projected_rows = jnp.dot(hidden_one, w_qkv, preferred_element_type=jnp.float32)
    cosine_values, sine_values = rope_tables(positions)

    def apply_rotation(tensor, heads):
        tensor = tensor.reshape(SEQUENCE_TOKENS, heads, HEAD_SIZE)
        return tensor * cosine_values[:, None, :] + rotate(tensor) * sine_values[:, None, :]

    def reverse_rotation(tensor):
        return tensor * cosine_values[:, None, :] - rotate(tensor) * sine_values[:, None, :]
    query_rows = rounded_values(apply_rotation(projected_rows[:, :query_total_width], QUERY_HEADS)).reshape(SEQUENCE_TOKENS, KEY_VALUE_HEADS, repeat_factor, HEAD_SIZE)
    key_row_slice = rounded_values(apply_rotation(projected_rows[:, query_total_width:query_total_width + key_value_width], KEY_VALUE_HEADS))
    value_row_slice = rounded_values(projected_rows[:, query_total_width + key_value_width:].reshape(SEQUENCE_TOKENS, KEY_VALUE_HEADS, HEAD_SIZE))
    attended_nat, lse_nat = attention_forward(natural(query_rows), natural(key_row_slice), natural(value_row_slice))
    attended_rows = attended_nat[positions].reshape(SEQUENCE_TOKENS, query_total_width)
    resid_mid = resid_in + jnp.dot(attended_rows, w_out, preferred_element_type=jnp.float32)
    scale_two = lax.rsqrt(lax.optimization_barrier(jnp.mean(resid_mid * resid_mid, axis=-1, keepdims=True)) + EPSILON)
    normed_two = resid_mid * scale_two
    hidden_two = (normed_two * gain_mlp).astype(jnp.bfloat16)
    gate_pre = jnp.dot(hidden_two, w_gate, preferred_element_type=jnp.float32)
    up_pre = jnp.dot(hidden_two, w_up, preferred_element_type=jnp.float32)
    sigmoid_gate = jax.nn.sigmoid(gate_pre)
    activated = (gate_pre * sigmoid_gate * up_pre).astype(jnp.bfloat16)
    mlp_delta = jnp.dot(activated, w_down, preferred_element_type=jnp.float32)
    layer_out = (resid_mid + mlp_delta).astype(jnp.bfloat16)
    act_grad = jnp.dot(cot_rows, w_down.T, preferred_element_type=jnp.float32)
    gate_grad = (act_grad * up_pre * sigmoid_gate * (1.0 + gate_pre * (1.0 - sigmoid_gate))).astype(jnp.bfloat16)
    up_grad = (act_grad * gate_pre * sigmoid_gate).astype(jnp.bfloat16)
    grad_down = jnp.dot(activated.T, cot_rows, preferred_element_type=jnp.float32)
    grad_gate = jnp.dot(hidden_two.T, gate_grad, preferred_element_type=jnp.float32)
    grad_up = jnp.dot(hidden_two.T, up_grad, preferred_element_type=jnp.float32)
    hidden_two_grad = jnp.dot(gate_grad, w_gate.T, preferred_element_type=jnp.float32) + jnp.dot(up_grad, w_up.T, preferred_element_type=jnp.float32)
    grad_gain_mlp = lax.optimization_barrier(jnp.sum(hidden_two_grad * normed_two, axis=0))
    norm_two_grad = hidden_two_grad * gain_mlp
    mid_grad = cot_rows.astype(jnp.float32) + scale_two * (norm_two_grad - normed_two * lax.optimization_barrier(jnp.mean(norm_two_grad * normed_two, axis=-1, keepdims=True)))
    mid_rounded = mid_grad.astype(jnp.bfloat16)
    grad_out = jnp.dot(attended_rows.T, mid_rounded, preferred_element_type=jnp.float32)
    attended_gradient = rounded_values(jnp.dot(mid_rounded, w_out.T, preferred_element_type=jnp.float32))
    attended_gradient = attended_gradient.reshape(SEQUENCE_TOKENS, KEY_VALUE_HEADS, repeat_factor, HEAD_SIZE)
    query_nat, key_nat, value_nat = attention_backward(natural(query_rows), natural(key_row_slice), natural(value_row_slice), attended_nat, natural(attended_gradient), lse_nat)
    query_gradient = query_nat[positions]
    key_gradient = key_nat[positions]
    value_gradient = value_nat[positions]
    proj_grad = jnp.concatenate([reverse_rotation(query_gradient).reshape(SEQUENCE_TOKENS, query_total_width), reverse_rotation(key_gradient).reshape(SEQUENCE_TOKENS, key_value_width), value_gradient.reshape(SEQUENCE_TOKENS, key_value_width)], axis=1).astype(jnp.bfloat16)
    grad_qkv = jnp.dot(hidden_one.T, proj_grad, preferred_element_type=jnp.float32)
    hidden_one_grad = jnp.dot(proj_grad, w_qkv.T, preferred_element_type=jnp.float32)
    grad_gain_attn = lax.optimization_barrier(jnp.sum(hidden_one_grad * normed_one, axis=0))
    norm_one_grad = hidden_one_grad * gain_attn
    input_grad = mid_grad + scale_one * (norm_one_grad - normed_one * lax.optimization_barrier(jnp.mean(norm_one_grad * normed_one, axis=-1, keepdims=True)))
    return (layer_out, input_grad, grad_qkv, grad_out, grad_gate, grad_up, grad_down, grad_gain_attn, grad_gain_mlp)

def reference(layer_input, cotangent, w_qkv, w_out, w_gate, w_up, w_down, gain_attn, gain_mlp):
    outputs = []
    input_grads = []
    grad_sets = []
    for sequence in range(SEQS):
        result = one_sequence(layer_input[sequence], cotangent[sequence], w_qkv, w_out, w_gate, w_up, w_down, gain_attn, gain_mlp)
        outputs.append(result[0])
        input_grads.append(result[1])
        grad_sets.append(result[2:])
    totals = list(grad_sets[0])
    for another in grad_sets[1:]:
        totals = [current + further for current, further in zip(totals, another)]
    return (jnp.stack(outputs), jnp.stack(input_grads), totals[0], totals[1], totals[2], totals[3], totals[4], totals[5], totals[6])
```

```python
import jax
import jax.numpy as jnp
from jax import lax
from jax.experimental import pallas as pl
from jax.experimental.pallas import tpu as pltpu
from jax.sharding import PartitionSpec as P

QUERY_HEADS = 9
KEY_VALUE_HEADS = 3
HEAD_SIZE = 64


EPSILON = 1e-05
ROPE_BASE = 100000.0


def row_sums(partial_value):
    return lax.psum(partial_value, "wt")


def rope_tables(positions):
    half_dim = HEAD_SIZE // 2
    frequency = jnp.power(
        jnp.float32(ROPE_BASE), -jnp.arange(half_dim, dtype=jnp.float32) * 2.0 / HEAD_SIZE
    )
    angles = positions.astype(jnp.float32)[:, None] * frequency[None, :]
    angles = jnp.concatenate([angles, angles], axis=1)
    return (jnp.cos(angles), jnp.sin(angles))


def rotate(tensor):
    half_dim = tensor.shape[-1] // 2
    return jnp.concatenate([-tensor[..., half_dim:], tensor[..., :half_dim]], axis=-1)


def apply_rotation(tensor, cosine_values, sine_values):
    return tensor * cosine_values[:, None, :] + rotate(tensor) * sine_values[:, None, :]


def reverse_rotation(tensor, cosine_values, sine_values):
    return tensor * cosine_values[:, None, :] - rotate(tensor) * sine_values[:, None, :]


def select_group(values_in, group_index):
    return lax.dynamic_index_in_dim(values_in, group_index, 0, keepdims=False)


def fetch_block(kv_stack, source, row_start, key_tile):
    key_value_half = kv_stack.shape[2] // 2
    key_value_block = lax.dynamic_slice(
        kv_stack, (source, row_start, 0), (1, key_tile, kv_stack.shape[2])
    )[0]
    key_portion = key_value_block[:, :key_value_half].reshape(key_tile, KEY_VALUE_HEADS, HEAD_SIZE)
    value_portion = key_value_block[:, key_value_half:].reshape(
        key_tile, KEY_VALUE_HEADS, HEAD_SIZE
    )
    return (key_portion, value_portion)


def split_device(layer_input, cotangent, w_qkv, w_out, w_gate, w_up, w_down, gain_attn, gain_mlp):
    ctx_count = lax.axis_size("ctx")
    wt_count = lax.axis_size("wt")
    ctx_index = lax.axis_index("ctx")
    wt_index = lax.axis_index("wt")
    resid_in = layer_input[0].astype(jnp.float32)
    tok_rows, part_width = resid_in.shape
    full_width = part_width * wt_count
    local_rows = tok_rows // wt_count
    segment_rows = local_rows // 2
    block_rows = tok_rows // 2
    repeat_factor = QUERY_HEADS // KEY_VALUE_HEADS
    query_total_width = QUERY_HEADS * HEAD_SIZE
    key_value_width = KEY_VALUE_HEADS * HEAD_SIZE
    scale_one = lax.rsqrt(row_sums(jnp.sum(resid_in * resid_in, axis=1)) / full_width + EPSILON)[
        :, None
    ]
    normed_one = resid_in * scale_one
    hidden_one = (normed_one * gain_attn).astype(jnp.bfloat16)
    rows_in = hidden_one
    projected_rows = lax.psum_scatter(
        jnp.dot(rows_in, w_qkv, preferred_element_type=jnp.float32).astype(jnp.bfloat16),
        "wt",
        scatter_dimension=0,
        tiled=True,
    ).astype(jnp.float32)
    offsets = jnp.arange(segment_rows, dtype=jnp.int32)
    early_pos = ctx_index * block_rows + wt_index * segment_rows + offsets
    late_pos = (2 * ctx_count - 1 - ctx_index) * block_rows + wt_index * segment_rows + offsets
    query_pos = jnp.stack([early_pos, late_pos])
    cosine_values, sine_values = rope_tables(query_pos.reshape(local_rows))
    query_rows = apply_rotation(
        projected_rows[:, :query_total_width].reshape(local_rows, QUERY_HEADS, HEAD_SIZE),
        cosine_values,
        sine_values,
    )
    query_rows = query_rows.astype(jnp.bfloat16).reshape(
        2, segment_rows, KEY_VALUE_HEADS, repeat_factor, HEAD_SIZE
    )
    key_row_slice = apply_rotation(
        projected_rows[:, query_total_width : query_total_width + key_value_width].reshape(
            local_rows, KEY_VALUE_HEADS, HEAD_SIZE
        ),
        cosine_values,
        sine_values,
    )
    key_row_slice = key_row_slice.astype(jnp.bfloat16).reshape(local_rows, key_value_width)
    value_row_slice = projected_rows[:, query_total_width + key_value_width :].astype(jnp.bfloat16)
    kv_pair = jnp.concatenate([key_row_slice, value_row_slice], axis=1).reshape(
        2, segment_rows, 2 * key_value_width
    )
    kv_all = lax.all_gather(kv_pair, ("ctx", "wt"), axis=1, tiled=True)
    half_len = kv_all.shape[1]
    key_tile = min(1024, half_len)
    block_total = half_len // key_tile
    early_count = (ctx_index * block_rows + (wt_index + 1) * segment_rows - 1) // key_tile + 1
    late_count = (
        (ctx_count - 1 - ctx_index) * block_rows + (wt_index + 1) * segment_rows - 1
    ) // key_tile + 1
    turn_total = early_count + block_total + late_count

    def locate(turn_index):
        query_group = (turn_index >= early_count).astype(jnp.int32)
        late_turn = turn_index - early_count
        source = query_group * (late_turn >= block_total).astype(jnp.int32)
        block_index = jnp.where(
            query_group == 0,
            turn_index,
            jnp.where(source == 0, late_turn, 2 * block_total - 1 - late_turn),
        )
        row_start = block_index * key_tile
        key_index = row_start + jnp.arange(key_tile, dtype=jnp.int32)
        late_keys = (
            2 * ctx_count - 1 - key_index // block_rows
        ) * block_rows + key_index % block_rows
        key_pos = jnp.where(source == 0, key_index, late_keys)
        return (query_group, source, row_start, key_pos)

    def group_scores(kv_stack, turn_index):
        query_group, source, row_start, key_pos = locate(turn_index)
        key_portion, value_portion = fetch_block(kv_stack, source, row_start, key_tile)
        query_sel = select_group(query_rows, query_group)
        scores = (
            jnp.einsum("pgrd,kgd->pgrk", query_sel, key_portion, preferred_element_type=jnp.float32)
            * 0.125
        )
        key_mask = (key_pos[None, :] <= select_group(query_pos, query_group)[:, None])[
            :, None, None, :
        ]
        scores = jnp.where(key_mask, scores, -1e30)
        return (
            query_group,
            source,
            row_start,
            query_sel,
            key_portion,
            value_portion,
            scores,
            key_mask,
        )

    def forward_turn(turn_index, loop_state):
        running_max, running_sum, attended_acc = loop_state
        query_group, source, row_start, query_sel, key_portion, value_portion, scores, key_mask = (
            group_scores(kv_all, turn_index)
        )
        previous = select_group(running_max, query_group)
        updated = jnp.maximum(previous, jnp.max(scores, axis=-1))
        shrink = jnp.exp(previous - updated)
        weights = jnp.where(key_mask, jnp.exp(scores - updated[..., None]), 0.0)
        summed_exp = select_group(running_sum, query_group) * shrink + jnp.sum(weights, axis=-1)
        gained = select_group(attended_acc, query_group) * shrink[..., None] + jnp.einsum(
            "pgrk,kgd->pgrd",
            weights.astype(jnp.bfloat16),
            value_portion,
            preferred_element_type=jnp.float32,
        )
        return (
            lax.dynamic_update_index_in_dim(running_max, updated, query_group, 0),
            lax.dynamic_update_index_in_dim(running_sum, summed_exp, query_group, 0),
            lax.dynamic_update_index_in_dim(attended_acc, gained, query_group, 0),
        )

    statistic_shape = (2, segment_rows, KEY_VALUE_HEADS, repeat_factor)
    running_max, running_sum, attended_acc = lax.fori_loop(
        0,
        turn_total,
        forward_turn,
        (
            jnp.full(statistic_shape, -1e30, jnp.float32),
            jnp.zeros(statistic_shape, jnp.float32),
            jnp.zeros((2, segment_rows, KEY_VALUE_HEADS, repeat_factor, HEAD_SIZE), jnp.float32),
        ),
    )
    logsumexp_every = running_max + jnp.log(running_sum)
    attended_rows = (attended_acc / running_sum[..., None]).astype(jnp.bfloat16)
    attended_all = lax.all_gather(
        attended_rows.reshape(local_rows, query_total_width), "wt", axis=0, tiled=True
    )
    resid_mid = resid_in + jnp.dot(attended_all, w_out, preferred_element_type=jnp.float32)
    scale_two = lax.rsqrt(row_sums(jnp.sum(resid_mid * resid_mid, axis=1)) / full_width + EPSILON)[
        :, None
    ]
    normed_two = resid_mid * scale_two
    hidden_two = (normed_two * gain_mlp).astype(jnp.bfloat16)
    hidden_full = lax.all_gather(hidden_two, "wt", axis=1, tiled=True)
    gate_pre = jnp.dot(hidden_full, w_gate, preferred_element_type=jnp.float32)
    up_pre = jnp.dot(hidden_full, w_up, preferred_element_type=jnp.float32)
    sigmoid_gate = jax.nn.sigmoid(gate_pre)
    activated = (gate_pre * sigmoid_gate * up_pre).astype(jnp.bfloat16)
    down_terms = jnp.dot(activated, w_down, preferred_element_type=jnp.float32)
    mlp_delta = lax.psum_scatter(
        down_terms.astype(jnp.bfloat16), "wt", scatter_dimension=1, tiled=True
    ).astype(jnp.float32)
    layer_out = (resid_mid + mlp_delta).astype(jnp.bfloat16)
    cot_rows = cotangent[0]
    cot_full = lax.all_gather(cot_rows, "wt", axis=1, tiled=True)
    act_grad = jnp.dot(cot_full, w_down.T, preferred_element_type=jnp.float32)
    gate_grad = (act_grad * up_pre * sigmoid_gate * (1.0 + gate_pre * (1.0 - sigmoid_gate))).astype(
        jnp.bfloat16
    )
    up_grad = (act_grad * gate_pre * sigmoid_gate).astype(jnp.bfloat16)
    grad_down = jnp.dot(activated.T, cot_full, preferred_element_type=jnp.float32)
    grad_gate = jnp.dot(hidden_full.T, gate_grad, preferred_element_type=jnp.float32)
    grad_up = jnp.dot(hidden_full.T, up_grad, preferred_element_type=jnp.float32)
    hidden_terms = jnp.dot(gate_grad, w_gate.T, preferred_element_type=jnp.float32) + jnp.dot(
        up_grad, w_up.T, preferred_element_type=jnp.float32
    )
    hidden_two_grad = lax.psum_scatter(
        hidden_terms.astype(jnp.bfloat16), "wt", scatter_dimension=1, tiled=True
    ).astype(jnp.float32)
    grad_gain_mlp = jnp.sum(hidden_two_grad * normed_two, axis=0)
    norm_two_grad = hidden_two_grad * gain_mlp
    mean_two = row_sums(jnp.sum(norm_two_grad * normed_two, axis=1)) / full_width
    mid_grad = cot_rows.astype(jnp.float32) + scale_two * (
        norm_two_grad - normed_two * mean_two[:, None]
    )
    mid_rounded = mid_grad.astype(jnp.bfloat16)
    grad_out = jnp.dot(attended_all.T, mid_rounded, preferred_element_type=jnp.float32)
    rows_in = mid_rounded
    attended_gradient = lax.psum_scatter(
        jnp.dot(rows_in, w_out.T, preferred_element_type=jnp.float32).astype(jnp.bfloat16),
        "wt",
        scatter_dimension=0,
        tiled=True,
    )
    attended_gradient = attended_gradient.reshape(
        2, segment_rows, KEY_VALUE_HEADS, repeat_factor, HEAD_SIZE
    )
    row_delta = jnp.sum(
        attended_gradient.astype(jnp.float32) * attended_rows.astype(jnp.float32), axis=-1
    )
    kv_reused = lax.all_gather(kv_pair, ("ctx", "wt"), axis=1, tiled=True)

    def back_turn(turn_index, loop_state):
        query_acc, kv_acc = loop_state
        query_group, source, row_start, query_sel, key_portion, value_portion, scores, key_mask = (
            group_scores(kv_reused, turn_index)
        )
        grad_sel = select_group(attended_gradient, query_group)
        probs_full = jnp.exp(scores - select_group(logsumexp_every, query_group)[..., None])
        prob_grad = jnp.einsum(
            "pgrd,kgd->pgrk", grad_sel, value_portion, preferred_element_type=jnp.float32
        )
        score_grad = (
            probs_full * (prob_grad - select_group(row_delta, query_group)[..., None])
        ).astype(jnp.bfloat16)
        weight_bf = probs_full.astype(jnp.bfloat16)
        query_new = (
            select_group(query_acc, query_group)
            + jnp.einsum(
                "pgrk,kgd->pgrd", score_grad, key_portion, preferred_element_type=jnp.float32
            )
            * 0.125
        )
        key_part_grad = (
            jnp.einsum("pgrk,pgrd->kgd", score_grad, query_sel, preferred_element_type=jnp.float32)
            * 0.125
        )
        value_part_grad = jnp.einsum(
            "pgrk,pgrd->kgd", weight_bf, grad_sel, preferred_element_type=jnp.float32
        )
        update_rows = jnp.concatenate(
            [
                key_part_grad.reshape(key_tile, key_value_width),
                value_part_grad.reshape(key_tile, key_value_width),
            ],
            axis=1,
        )[None]
        previous = lax.dynamic_slice(kv_acc, (source, row_start, 0), update_rows.shape)
        kv_acc = lax.dynamic_update_slice(kv_acc, previous + update_rows, (source, row_start, 0))
        return (lax.dynamic_update_index_in_dim(query_acc, query_new, query_group, 0), kv_acc)

    query_acc, kv_acc = lax.fori_loop(
        0,
        turn_total,
        back_turn,
        (
            jnp.zeros((2, segment_rows, KEY_VALUE_HEADS, repeat_factor, HEAD_SIZE), jnp.float32),
            jnp.zeros((2, half_len, 2 * key_value_width), jnp.float32),
        ),
    )
    key_value_gradient = lax.psum_scatter(
        kv_acc, ("ctx", "wt"), scatter_dimension=1, tiled=True
    ).reshape(local_rows, 2 * key_value_width)
    query_gradient = reverse_rotation(
        query_acc.reshape(local_rows, QUERY_HEADS, HEAD_SIZE), cosine_values, sine_values
    )
    key_gradient = reverse_rotation(
        key_value_gradient[:, :key_value_width].reshape(local_rows, KEY_VALUE_HEADS, HEAD_SIZE),
        cosine_values,
        sine_values,
    )
    proj_grad = jnp.concatenate(
        [
            query_gradient.reshape(local_rows, query_total_width),
            key_gradient.reshape(local_rows, key_value_width),
            key_value_gradient[:, key_value_width:],
        ],
        axis=1,
    ).astype(jnp.bfloat16)
    proj_all = lax.all_gather(proj_grad, "wt", axis=0, tiled=True)
    grad_qkv = jnp.dot(hidden_one.T, proj_all, preferred_element_type=jnp.float32)
    hidden_one_grad = jnp.dot(proj_all, w_qkv.T, preferred_element_type=jnp.float32)
    grad_gain_attn = jnp.sum(hidden_one_grad * normed_one, axis=0)
    norm_one_grad = hidden_one_grad * gain_attn
    mean_one = row_sums(jnp.sum(norm_one_grad * normed_one, axis=1)) / full_width
    input_grad = mid_grad + scale_one * (norm_one_grad - normed_one * mean_one[:, None])
    summed = lax.psum(
        (grad_qkv, grad_out, grad_gate, grad_up, grad_down, grad_gain_attn, grad_gain_mlp),
        ("seq", "ctx"),
    )
    return (
        layer_out[None],
        input_grad[None],
        summed[0],
        summed[1],
        summed[2],
        summed[3],
        summed[4],
        summed[5],
        summed[6],
    )


ROW_TILE = 256
NT = (((1,), (1,)), ((), ()))
TN = (((0,), (0,)), ((), ()))
BF = jnp.bfloat16
F32 = jnp.float32


def swap(value, axis, distance, count):
    return lax.ppermute(value, axis, [(i, i ^ distance) for i in range(count)])


def gather_blocks(block, ctx_count):
    rows = [block] + [swap(block, "ctx", d, ctx_count) for d in range(2, ctx_count, 2)]
    near = [swap(part, "ctx", 1, ctx_count) for part in rows]
    across = [swap(part, "wt", 1, 2) for part in rows]
    half = len(rows) // 2
    corner = [swap(part, "wt", 1, 2) for part in near[:half]]
    corner += [swap(part, "ctx", 1, ctx_count) for part in across[half:]]
    found = []
    for k in range(len(rows)):
        found.append((2 * k, rows[k], across[k]))
        found.append((2 * k + 1, near[k], corner[k]))
    return found


def in_order(own, other, wt_index, axis):
    return jnp.where(
        wt_index == 0,
        jnp.concatenate([own, other], axis=axis),
        jnp.concatenate([other, own], axis=axis),
    )


def place_kernel(distances, where_ref, *refs):
    blocks, out = refs[:-1], refs[-1]
    ctx, wt = where_ref[0], where_ref[1]
    last = 2 * len(distances) - 1
    piece = blocks[0].shape[0] // 4
    for k, distance in enumerate(distances):
        owner = jnp.bitwise_xor(ctx, distance)
        full = in_order(blocks[2 * k][...], blocks[2 * k + 1][...], wt, 1)
        for j in range(4):
            base = owner if j % 2 == 0 else last - owner
            start = pl.multiple_of(base * (2 * piece) + (j // 2) * piece, piece)
            out[pl.ds(start, piece), :] = full[j * piece : (j + 1) * piece]


def place(found, where):
    distances = [d for d, _, _ in found]
    blocks = [b for _, own, other in found for b in (own, other)]
    rows, width = blocks[0].shape
    vmem = pl.BlockSpec(memory_space=pltpu.VMEM)
    return pl.pallas_call(
        lambda *refs: place_kernel(distances, *refs),
        in_specs=[pl.BlockSpec(memory_space=pltpu.SMEM)] + [vmem] * len(blocks),
        out_specs=vmem,
        out_shape=jax.ShapeDtypeStruct((rows * len(found), 2 * width), blocks[0].dtype),
        name="place",
    )(where, *blocks)


def turned(value):
    return value.astype(F32).T.astype(BF)


def attend_kernel(q_ref, k_ref, v_ref, out_ref, lse_ref):
    rows = q_ref.shape[1]
    keys = turned(k_ref[...])
    tile = min(ROW_TILE, rows)
    for start in range(0, rows, tile):
        stop = start + tile
        scores = jnp.dot(keys[:stop], q_ref[:, start:stop], preferred_element_type=F32) * 0.125
        key_at = lax.broadcasted_iota(jnp.int32, scores.shape, 0)
        row_at = lax.broadcasted_iota(jnp.int32, scores.shape, 1) + start
        scores = jnp.where(key_at <= row_at, scores, -1e30)
        top = jnp.max(scores, axis=0, keepdims=True)
        weights = jnp.exp(scores - top)
        total = jnp.sum(weights, axis=0, keepdims=True)
        out = jnp.dot(v_ref[:, :stop], weights.astype(BF), preferred_element_type=F32)
        out_ref[:, start:stop] = (out / total).astype(BF)
        lse_ref[0, :, start:stop] = top + jnp.log(total)


def attend_back_kernel(q_ref, k_ref, v_ref, g_ref, o_ref, lse_ref, dq_ref, dk_ref, dv_ref):
    rows = q_ref.shape[1]
    tile = min(ROW_TILE, rows)
    keys, values = turned(k_ref[...]), turned(v_ref[...])

    @pl.when(pl.program_id(0) % (QUERY_HEADS // KEY_VALUE_HEADS) == 0)
    def _():
        dk_ref[...] = jnp.zeros_like(dk_ref)
        dv_ref[...] = jnp.zeros_like(dv_ref)

    delta = jnp.sum(g_ref[...].astype(F32) * o_ref[...].astype(F32), axis=0, keepdims=True)
    for start in range(0, rows, tile):
        stop = start + tile
        scores = jnp.dot(keys[:stop], q_ref[:, start:stop], preferred_element_type=F32) * 0.125
        key_at = lax.broadcasted_iota(jnp.int32, scores.shape, 0)
        row_at = lax.broadcasted_iota(jnp.int32, scores.shape, 1) + start
        scores = jnp.where(key_at <= row_at, scores, -1e30)
        probs = jnp.exp(scores - lse_ref[0, :, start:stop])
        prob_grad = jnp.dot(values[:stop], g_ref[:, start:stop], preferred_element_type=F32)
        score_grad = (probs * (prob_grad - delta[:, start:stop])).astype(BF)
        probs = probs.astype(BF)
        dq = jnp.dot(k_ref[:, :stop], score_grad, preferred_element_type=F32)
        dq_ref[:, start:stop] = dq * 0.125
        dk = lax.dot_general(q_ref[:, start:stop], score_grad, NT, preferred_element_type=F32)
        dk_ref[:, :stop] += dk * 0.125
        dv = lax.dot_general(g_ref[:, start:stop], probs, NT, preferred_element_type=F32)
        dv_ref[:, :stop] += dv


def attend_specs(rows):
    repeat = QUERY_HEADS // KEY_VALUE_HEADS
    query = pl.BlockSpec((HEAD_SIZE, rows), lambda h: (h, 0))
    pair = pl.BlockSpec((HEAD_SIZE, rows), lambda h: (h // repeat, 0))
    stat = pl.BlockSpec((1, 1, rows), lambda h: (h, 0, 0))
    return query, pair, stat


def attend(q_t, k_t, v_t):
    rows = q_t.shape[1]
    query, pair, stat = attend_specs(rows)
    return pl.pallas_call(
        attend_kernel,
        grid=(QUERY_HEADS,),
        in_specs=[query, pair, pair],
        out_specs=[query, stat],
        out_shape=[
            jax.ShapeDtypeStruct(q_t.shape, BF),
            jax.ShapeDtypeStruct((QUERY_HEADS, 1, rows), F32),
        ],
        name="attend",
    )(q_t, k_t, v_t)


def attend_back(q_t, k_t, v_t, g_t, o_t, lse):
    rows = q_t.shape[1]
    query, pair, stat = attend_specs(rows)
    return pl.pallas_call(
        attend_back_kernel,
        grid=(QUERY_HEADS,),
        in_specs=[query, pair, pair, query, query, stat],
        out_specs=[query, pair, pair],
        out_shape=[
            jax.ShapeDtypeStruct(q_t.shape, F32),
            jax.ShapeDtypeStruct(k_t.shape, F32),
            jax.ShapeDtypeStruct(k_t.shape, F32),
        ],
        name="attend_back",
    )(q_t, k_t, v_t, g_t, o_t, lse)


def both_sequences(value):
    mine = value.astype(BF)
    return mine.astype(F32) + swap(mine, "seq", 1, 2).astype(F32)


def whole_device(layer_input, cotangent, w_qkv, w_out, w_gate, w_up, w_down, gain_attn, gain_mlp):
    ctx_count = lax.axis_size("ctx")
    ctx_index = lax.axis_index("ctx")
    wt_index = lax.axis_index("wt")
    seq_index = lax.axis_index("seq")
    where = jnp.stack([ctx_index, wt_index]).astype(jnp.int32)
    tok_rows, part_width = layer_input.shape[1:]
    full_width = 2 * part_width
    rows = tok_rows * ctx_count
    block_rows = tok_rows // 2
    query_width = QUERY_HEADS * HEAD_SIZE
    pair_width = KEY_VALUE_HEADS * HEAD_SIZE
    hidden = w_gate.shape[1]

    def other_shard(value):
        half = value.shape[0] // 2
        mine = lax.dynamic_slice_in_dim(value, seq_index * half, half, 0)
        first = swap(mine, "wt", 1, 2)
        second = swap(first, "seq", 1, 2)
        return first, second

    def other_rows(value):
        first, second = other_shard(value)
        return in_order(first, second, seq_index, 0)

    def mine_of(value):
        early = lax.dynamic_slice_in_dim(value, ctx_index * block_rows, block_rows, 0)
        late_at = (2 * ctx_count - 1 - ctx_index) * block_rows
        late = lax.dynamic_slice_in_dim(value, late_at, block_rows, 0)
        both = jnp.stack([early, late]).reshape(2, 2, block_rows // 2, value.shape[1])
        return both.transpose(1, 0, 2, 3).reshape(tok_rows, value.shape[1])

    def my_columns(value):
        return lax.dynamic_slice_in_dim(value, wt_index * part_width, part_width, 1)

    gains = jnp.stack([gain_attn, gain_mlp])
    gains = in_order(gains, swap(gains, "wt", 1, 2), wt_index, 1)
    gain_one, gain_two = gains[0:1], gains[1:2]
    qkv_full = in_order(w_qkv, other_rows(w_qkv), wt_index, 0)
    found = gather_blocks(layer_input[0], ctx_count)
    inputs = place(found, where)
    out_full = in_order(w_out, other_rows(w_out), wt_index, 1)
    gate_full = jnp.concatenate([w_gate, other_rows(w_gate)], axis=1)
    up_full = jnp.concatenate([w_up, other_rows(w_up)], axis=1)
    down_full = jnp.concatenate([w_down, other_rows(w_down)], axis=0)
    cots = place(gather_blocks(cotangent[0], ctx_count), where)

    resid_in = inputs.astype(F32)
    scale_one = lax.rsqrt(jnp.mean(resid_in * resid_in, axis=1, keepdims=True) + EPSILON)
    normed_one = resid_in * scale_one
    hidden_one = (normed_one * gain_one).astype(BF)
    projected = lax.dot_general(
        qkv_full, hidden_one, (((0,), (1,)), ((), ())), preferred_element_type=F32
    )
    half_dim = HEAD_SIZE // 2
    frequency = jnp.power(F32(ROPE_BASE), -jnp.arange(half_dim, dtype=F32) * 2.0 / HEAD_SIZE)
    angles = frequency[:, None] * jnp.arange(rows, dtype=F32)[None, :]
    cosines, sines = jnp.cos(angles), jnp.sin(angles)

    def turn(value, sign):
        heads = value.reshape(-1, 2, half_dim, rows)
        first, second = heads[:, 0], heads[:, 1]
        low = first * cosines - sign * second * sines
        high = second * cosines + sign * first * sines
        return jnp.stack([low, high], axis=1).reshape(value.shape)

    turned_rows = turn(projected[: query_width + pair_width], 1.0).astype(BF)
    q_t, k_t = turned_rows[:query_width], turned_rows[query_width:]
    v_t = projected[query_width + pair_width :].astype(BF)
    attended_t, lse = attend(q_t, k_t, v_t)
    resid_mid = resid_in + lax.dot_general(attended_t, out_full, TN, preferred_element_type=F32)
    scale_two = lax.rsqrt(jnp.mean(resid_mid * resid_mid, axis=1, keepdims=True) + EPSILON)
    normed_two = resid_mid * scale_two
    hidden_two = (normed_two * gain_two).astype(BF)
    gate_pre = jnp.dot(hidden_two, gate_full, preferred_element_type=F32)
    up_pre = jnp.dot(hidden_two, up_full, preferred_element_type=F32)
    sigmoid_gate = jax.nn.sigmoid(gate_pre)
    activated = (gate_pre * sigmoid_gate * up_pre).astype(BF)
    mlp_delta = jnp.dot(mine_of(activated), my_columns(down_full), preferred_element_type=F32)
    layer_out = (mine_of(my_columns(resid_mid)) + mlp_delta).astype(BF)
    act_grad = lax.dot_general(cots, down_full, NT, preferred_element_type=F32)
    gate_grad = (
        act_grad * up_pre * sigmoid_gate * (1.0 + gate_pre * (1.0 - sigmoid_gate))
    ).astype(BF)
    up_grad = (act_grad * gate_pre * sigmoid_gate).astype(BF)
    grad_down = lax.dot_general(activated[:, :hidden], cots, TN, preferred_element_type=F32)
    grad_gate = lax.dot_general(hidden_two, gate_grad[:, :hidden], TN, preferred_element_type=F32)
    grad_up = lax.dot_general(hidden_two, up_grad[:, :hidden], TN, preferred_element_type=F32)
    grad_down, grad_gate, grad_up = map(both_sequences, (grad_down, grad_gate, grad_up))
    hidden_two_grad = lax.dot_general(gate_grad, gate_full, NT, preferred_element_type=F32)
    hidden_two_grad += lax.dot_general(up_grad, up_full, NT, preferred_element_type=F32)
    gain_two_part = jnp.sum(hidden_two_grad * normed_two, axis=0, keepdims=True)
    norm_grad = hidden_two_grad * gain_two
    mean_two = jnp.mean(norm_grad * normed_two, axis=1, keepdims=True)
    mid_grad = cots.astype(F32) + scale_two * (norm_grad - normed_two * mean_two)
    mid_rounded = mid_grad.astype(BF)
    grad_out = jnp.dot(attended_t, my_columns(mid_rounded), preferred_element_type=F32)
    grad_out = both_sequences(grad_out)
    g_t = lax.dot_general(out_full, mid_rounded, NT, preferred_element_type=F32).astype(BF)
    dq, dk, dv = attend_back(q_t, k_t, v_t, g_t, attended_t, lse)
    proj_grad = jnp.concatenate([turn(dq, -1.0), turn(dk, -1.0), dv], axis=0).astype(BF)
    grad_qkv = lax.dot_general(
        my_columns(hidden_one), proj_grad, (((0,), (1,)), ((), ())), preferred_element_type=F32
    )
    grad_qkv = both_sequences(grad_qkv)
    hidden_one_grad = lax.dot_general(
        proj_grad, qkv_full, (((0,), (1,)), ((), ())), preferred_element_type=F32
    )
    gain_one_part = jnp.sum(hidden_one_grad * normed_one, axis=0, keepdims=True)
    norm_grad = hidden_one_grad * gain_one
    mean_one = jnp.mean(norm_grad * normed_one, axis=1, keepdims=True)
    input_grad = mid_grad + scale_one * (norm_grad - normed_one * mean_one)
    input_grad = mine_of(my_columns(input_grad))
    gain_parts = my_columns(jnp.concatenate([gain_one_part, gain_two_part], axis=0))
    gain_parts = gain_parts + swap(gain_parts, "seq", 1, 2)
    return (
        layer_out[None],
        input_grad[None],
        grad_qkv,
        grad_out,
        grad_gate,
        grad_up,
        grad_down,
        gain_parts[0],
        gain_parts[1],
    )


def solution(mesh):
    in_specs = (
        P("seq", "ctx", "wt"),
        P("seq", "ctx", "wt"),
        P("wt", None),
        P(None, "wt"),
        P(None, "wt"),
        P(None, "wt"),
        P("wt", None),
        P("wt"),
        P("wt"),
    )
    out_specs = (
        P("seq", "ctx", "wt"),
        P("seq", "ctx", "wt"),
        P("wt", None),
        P(None, "wt"),
        P(None, "wt"),
        P(None, "wt"),
        P("wt", None),
        P("wt"),
        P("wt"),
    )
    sizes = mesh.shape
    whole = sizes["wt"] == 2 and sizes["seq"] == 2 and sizes["ctx"] in (2, 4, 8)
    return jax.shard_map(
        whole_device if whole else split_device, mesh=mesh, in_specs=in_specs, out_specs=out_specs, check_vma=False
    )
```

```python
import jax
import jax.numpy as jnp
from jax import lax
from jax.experimental import pallas as pl
from jax.experimental.pallas import tpu as pltpu
from jax.sharding import PartitionSpec as P

QUERY_HEADS = 9
KEY_VALUE_HEADS = 3
HEAD_SIZE = 64


EPSILON = 1e-05
ROPE_BASE = 100000.0


def row_sums(partial_value):
    return lax.psum(partial_value, "wt")


def rope_tables(positions):
    half_dim = HEAD_SIZE // 2
    frequency = jnp.power(
        jnp.float32(ROPE_BASE), -jnp.arange(half_dim, dtype=jnp.float32) * 2.0 / HEAD_SIZE
    )
    angles = positions.astype(jnp.float32)[:, None] * frequency[None, :]
    angles = jnp.concatenate([angles, angles], axis=1)
    return (jnp.cos(angles), jnp.sin(angles))


def rotate(tensor):
    half_dim = tensor.shape[-1] // 2
    return jnp.concatenate([-tensor[..., half_dim:], tensor[..., :half_dim]], axis=-1)


def apply_rotation(tensor, cosine_values, sine_values):
    return tensor * cosine_values[:, None, :] + rotate(tensor) * sine_values[:, None, :]


def reverse_rotation(tensor, cosine_values, sine_values):
    return tensor * cosine_values[:, None, :] - rotate(tensor) * sine_values[:, None, :]


def select_group(values_in, group_index):
    return lax.dynamic_index_in_dim(values_in, group_index, 0, keepdims=False)


def fetch_block(kv_stack, source, row_start, key_tile):
    key_value_half = kv_stack.shape[2] // 2
    key_value_block = lax.dynamic_slice(
        kv_stack, (source, row_start, 0), (1, key_tile, kv_stack.shape[2])
    )[0]
    key_portion = key_value_block[:, :key_value_half].reshape(key_tile, KEY_VALUE_HEADS, HEAD_SIZE)
    value_portion = key_value_block[:, key_value_half:].reshape(
        key_tile, KEY_VALUE_HEADS, HEAD_SIZE
    )
    return (key_portion, value_portion)


def split_device(layer_input, cotangent, w_qkv, w_out, w_gate, w_up, w_down, gain_attn, gain_mlp):
    ctx_count = lax.axis_size("ctx")
    wt_count = lax.axis_size("wt")
    ctx_index = lax.axis_index("ctx")
    wt_index = lax.axis_index("wt")
    resid_in = layer_input[0].astype(jnp.float32)
    tok_rows, part_width = resid_in.shape
    full_width = part_width * wt_count
    local_rows = tok_rows // wt_count
    segment_rows = local_rows // 2
    block_rows = tok_rows // 2
    repeat_factor = QUERY_HEADS // KEY_VALUE_HEADS
    query_total_width = QUERY_HEADS * HEAD_SIZE
    key_value_width = KEY_VALUE_HEADS * HEAD_SIZE
    scale_one = lax.rsqrt(row_sums(jnp.sum(resid_in * resid_in, axis=1)) / full_width + EPSILON)[
        :, None
    ]
    normed_one = resid_in * scale_one
    hidden_one = (normed_one * gain_attn).astype(jnp.bfloat16)
    rows_in = hidden_one
    projected_rows = lax.psum_scatter(
        jnp.dot(rows_in, w_qkv, preferred_element_type=jnp.float32).astype(jnp.bfloat16),
        "wt",
        scatter_dimension=0,
        tiled=True,
    ).astype(jnp.float32)
    offsets = jnp.arange(segment_rows, dtype=jnp.int32)
    early_pos = ctx_index * block_rows + wt_index * segment_rows + offsets
    late_pos = (2 * ctx_count - 1 - ctx_index) * block_rows + wt_index * segment_rows + offsets
    query_pos = jnp.stack([early_pos, late_pos])
    cosine_values, sine_values = rope_tables(query_pos.reshape(local_rows))
    query_rows = apply_rotation(
        projected_rows[:, :query_total_width].reshape(local_rows, QUERY_HEADS, HEAD_SIZE),
        cosine_values,
        sine_values,
    )
    query_rows = query_rows.astype(jnp.bfloat16).reshape(
        2, segment_rows, KEY_VALUE_HEADS, repeat_factor, HEAD_SIZE
    )
    key_row_slice = apply_rotation(
        projected_rows[:, query_total_width : query_total_width + key_value_width].reshape(
            local_rows, KEY_VALUE_HEADS, HEAD_SIZE
        ),
        cosine_values,
        sine_values,
    )
    key_row_slice = key_row_slice.astype(jnp.bfloat16).reshape(local_rows, key_value_width)
    value_row_slice = projected_rows[:, query_total_width + key_value_width :].astype(jnp.bfloat16)
    kv_pair = jnp.concatenate([key_row_slice, value_row_slice], axis=1).reshape(
        2, segment_rows, 2 * key_value_width
    )
    kv_all = lax.all_gather(kv_pair, ("ctx", "wt"), axis=1, tiled=True)
    half_len = kv_all.shape[1]
    key_tile = min(1024, half_len)
    block_total = half_len // key_tile
    early_count = (ctx_index * block_rows + (wt_index + 1) * segment_rows - 1) // key_tile + 1
    late_count = (
        (ctx_count - 1 - ctx_index) * block_rows + (wt_index + 1) * segment_rows - 1
    ) // key_tile + 1
    turn_total = early_count + block_total + late_count

    def locate(turn_index):
        query_group = (turn_index >= early_count).astype(jnp.int32)
        late_turn = turn_index - early_count
        source = query_group * (late_turn >= block_total).astype(jnp.int32)
        block_index = jnp.where(
            query_group == 0,
            turn_index,
            jnp.where(source == 0, late_turn, 2 * block_total - 1 - late_turn),
        )
        row_start = block_index * key_tile
        key_index = row_start + jnp.arange(key_tile, dtype=jnp.int32)
        late_keys = (
            2 * ctx_count - 1 - key_index // block_rows
        ) * block_rows + key_index % block_rows
        key_pos = jnp.where(source == 0, key_index, late_keys)
        return (query_group, source, row_start, key_pos)

    def group_scores(kv_stack, turn_index):
        query_group, source, row_start, key_pos = locate(turn_index)
        key_portion, value_portion = fetch_block(kv_stack, source, row_start, key_tile)
        query_sel = select_group(query_rows, query_group)
        scores = (
            jnp.einsum("pgrd,kgd->pgrk", query_sel, key_portion, preferred_element_type=jnp.float32)
            * 0.125
        )
        key_mask = (key_pos[None, :] <= select_group(query_pos, query_group)[:, None])[
            :, None, None, :
        ]
        scores = jnp.where(key_mask, scores, -1e30)
        return (
            query_group,
            source,
            row_start,
            query_sel,
            key_portion,
            value_portion,
            scores,
            key_mask,
        )

    def forward_turn(turn_index, loop_state):
        running_max, running_sum, attended_acc = loop_state
        query_group, source, row_start, query_sel, key_portion, value_portion, scores, key_mask = (
            group_scores(kv_all, turn_index)
        )
        previous = select_group(running_max, query_group)
        updated = jnp.maximum(previous, jnp.max(scores, axis=-1))
        shrink = jnp.exp(previous - updated)
        weights = jnp.where(key_mask, jnp.exp(scores - updated[..., None]), 0.0)
        summed_exp = select_group(running_sum, query_group) * shrink + jnp.sum(weights, axis=-1)
        gained = select_group(attended_acc, query_group) * shrink[..., None] + jnp.einsum(
            "pgrk,kgd->pgrd",
            weights.astype(jnp.bfloat16),
            value_portion,
            preferred_element_type=jnp.float32,
        )
        return (
            lax.dynamic_update_index_in_dim(running_max, updated, query_group, 0),
            lax.dynamic_update_index_in_dim(running_sum, summed_exp, query_group, 0),
            lax.dynamic_update_index_in_dim(attended_acc, gained, query_group, 0),
        )

    statistic_shape = (2, segment_rows, KEY_VALUE_HEADS, repeat_factor)
    running_max, running_sum, attended_acc = lax.fori_loop(
        0,
        turn_total,
        forward_turn,
        (
            jnp.full(statistic_shape, -1e30, jnp.float32),
            jnp.zeros(statistic_shape, jnp.float32),
            jnp.zeros((2, segment_rows, KEY_VALUE_HEADS, repeat_factor, HEAD_SIZE), jnp.float32),
        ),
    )
    logsumexp_every = running_max + jnp.log(running_sum)
    attended_rows = (attended_acc / running_sum[..., None]).astype(jnp.bfloat16)
    attended_all = lax.all_gather(
        attended_rows.reshape(local_rows, query_total_width), "wt", axis=0, tiled=True
    )
    resid_mid = resid_in + jnp.dot(attended_all, w_out, preferred_element_type=jnp.float32)
    scale_two = lax.rsqrt(row_sums(jnp.sum(resid_mid * resid_mid, axis=1)) / full_width + EPSILON)[
        :, None
    ]
    normed_two = resid_mid * scale_two
    hidden_two = (normed_two * gain_mlp).astype(jnp.bfloat16)
    hidden_full = lax.all_gather(hidden_two, "wt", axis=1, tiled=True)
    gate_pre = jnp.dot(hidden_full, w_gate, preferred_element_type=jnp.float32)
    up_pre = jnp.dot(hidden_full, w_up, preferred_element_type=jnp.float32)
    sigmoid_gate = jax.nn.sigmoid(gate_pre)
    activated = (gate_pre * sigmoid_gate * up_pre).astype(jnp.bfloat16)
    down_terms = jnp.dot(activated, w_down, preferred_element_type=jnp.float32)
    mlp_delta = lax.psum_scatter(
        down_terms.astype(jnp.bfloat16), "wt", scatter_dimension=1, tiled=True
    ).astype(jnp.float32)
    layer_out = (resid_mid + mlp_delta).astype(jnp.bfloat16)
    cot_rows = cotangent[0]
    cot_full = lax.all_gather(cot_rows, "wt", axis=1, tiled=True)
    act_grad = jnp.dot(cot_full, w_down.T, preferred_element_type=jnp.float32)
    gate_grad = (act_grad * up_pre * sigmoid_gate * (1.0 + gate_pre * (1.0 - sigmoid_gate))).astype(
        jnp.bfloat16
    )
    up_grad = (act_grad * gate_pre * sigmoid_gate).astype(jnp.bfloat16)
    grad_down = jnp.dot(activated.T, cot_full, preferred_element_type=jnp.float32)
    grad_gate = jnp.dot(hidden_full.T, gate_grad, preferred_element_type=jnp.float32)
    grad_up = jnp.dot(hidden_full.T, up_grad, preferred_element_type=jnp.float32)
    hidden_terms = jnp.dot(gate_grad, w_gate.T, preferred_element_type=jnp.float32) + jnp.dot(
        up_grad, w_up.T, preferred_element_type=jnp.float32
    )
    hidden_two_grad = lax.psum_scatter(
        hidden_terms.astype(jnp.bfloat16), "wt", scatter_dimension=1, tiled=True
    ).astype(jnp.float32)
    grad_gain_mlp = jnp.sum(hidden_two_grad * normed_two, axis=0)
    norm_two_grad = hidden_two_grad * gain_mlp
    mean_two = row_sums(jnp.sum(norm_two_grad * normed_two, axis=1)) / full_width
    mid_grad = cot_rows.astype(jnp.float32) + scale_two * (
        norm_two_grad - normed_two * mean_two[:, None]
    )
    mid_rounded = mid_grad.astype(jnp.bfloat16)
    grad_out = jnp.dot(attended_all.T, mid_rounded, preferred_element_type=jnp.float32)
    rows_in = mid_rounded
    attended_gradient = lax.psum_scatter(
        jnp.dot(rows_in, w_out.T, preferred_element_type=jnp.float32).astype(jnp.bfloat16),
        "wt",
        scatter_dimension=0,
        tiled=True,
    )
    attended_gradient = attended_gradient.reshape(
        2, segment_rows, KEY_VALUE_HEADS, repeat_factor, HEAD_SIZE
    )
    row_delta = jnp.sum(
        attended_gradient.astype(jnp.float32) * attended_rows.astype(jnp.float32), axis=-1
    )
    kv_reused = lax.all_gather(kv_pair, ("ctx", "wt"), axis=1, tiled=True)

    def back_turn(turn_index, loop_state):
        query_acc, kv_acc = loop_state
        query_group, source, row_start, query_sel, key_portion, value_portion, scores, key_mask = (
            group_scores(kv_reused, turn_index)
        )
        grad_sel = select_group(attended_gradient, query_group)
        probs_full = jnp.exp(scores - select_group(logsumexp_every, query_group)[..., None])
        prob_grad = jnp.einsum(
            "pgrd,kgd->pgrk", grad_sel, value_portion, preferred_element_type=jnp.float32
        )
        score_grad = (
            probs_full * (prob_grad - select_group(row_delta, query_group)[..., None])
        ).astype(jnp.bfloat16)
        weight_bf = probs_full.astype(jnp.bfloat16)
        query_new = (
            select_group(query_acc, query_group)
            + jnp.einsum(
                "pgrk,kgd->pgrd", score_grad, key_portion, preferred_element_type=jnp.float32
            )
            * 0.125
        )
        key_part_grad = (
            jnp.einsum("pgrk,pgrd->kgd", score_grad, query_sel, preferred_element_type=jnp.float32)
            * 0.125
        )
        value_part_grad = jnp.einsum(
            "pgrk,pgrd->kgd", weight_bf, grad_sel, preferred_element_type=jnp.float32
        )
        update_rows = jnp.concatenate(
            [
                key_part_grad.reshape(key_tile, key_value_width),
                value_part_grad.reshape(key_tile, key_value_width),
            ],
            axis=1,
        )[None]
        previous = lax.dynamic_slice(kv_acc, (source, row_start, 0), update_rows.shape)
        kv_acc = lax.dynamic_update_slice(kv_acc, previous + update_rows, (source, row_start, 0))
        return (lax.dynamic_update_index_in_dim(query_acc, query_new, query_group, 0), kv_acc)

    query_acc, kv_acc = lax.fori_loop(
        0,
        turn_total,
        back_turn,
        (
            jnp.zeros((2, segment_rows, KEY_VALUE_HEADS, repeat_factor, HEAD_SIZE), jnp.float32),
            jnp.zeros((2, half_len, 2 * key_value_width), jnp.float32),
        ),
    )
    key_value_gradient = lax.psum_scatter(
        kv_acc, ("ctx", "wt"), scatter_dimension=1, tiled=True
    ).reshape(local_rows, 2 * key_value_width)
    query_gradient = reverse_rotation(
        query_acc.reshape(local_rows, QUERY_HEADS, HEAD_SIZE), cosine_values, sine_values
    )
    key_gradient = reverse_rotation(
        key_value_gradient[:, :key_value_width].reshape(local_rows, KEY_VALUE_HEADS, HEAD_SIZE),
        cosine_values,
        sine_values,
    )
    proj_grad = jnp.concatenate(
        [
            query_gradient.reshape(local_rows, query_total_width),
            key_gradient.reshape(local_rows, key_value_width),
            key_value_gradient[:, key_value_width:],
        ],
        axis=1,
    ).astype(jnp.bfloat16)
    proj_all = lax.all_gather(proj_grad, "wt", axis=0, tiled=True)
    grad_qkv = jnp.dot(hidden_one.T, proj_all, preferred_element_type=jnp.float32)
    hidden_one_grad = jnp.dot(proj_all, w_qkv.T, preferred_element_type=jnp.float32)
    grad_gain_attn = jnp.sum(hidden_one_grad * normed_one, axis=0)
    norm_one_grad = hidden_one_grad * gain_attn
    mean_one = row_sums(jnp.sum(norm_one_grad * normed_one, axis=1)) / full_width
    input_grad = mid_grad + scale_one * (norm_one_grad - normed_one * mean_one[:, None])
    summed = lax.psum(
        (grad_qkv, grad_out, grad_gate, grad_up, grad_down, grad_gain_attn, grad_gain_mlp),
        ("seq", "ctx"),
    )
    return (
        layer_out[None],
        input_grad[None],
        summed[0],
        summed[1],
        summed[2],
        summed[3],
        summed[4],
        summed[5],
        summed[6],
    )


FORWARD_TILE = 512
BACKWARD_TILE = 256
HIDDEN_TILE = 256
ROW_DISTANCES = (0, 4, 2, 6)
NN = (((1,), (0,)), ((), ()))
NT = (((1,), (1,)), ((), ()))
TN = (((0,), (0,)), ((), ()))
BF = jnp.bfloat16
F32 = jnp.float32
VMEM = pl.BlockSpec(memory_space=pltpu.VMEM)
SMEM = pl.BlockSpec(memory_space=pltpu.SMEM)
ANY = pl.BlockSpec(memory_space=pl.ANY)


def swap(value, axis, distance, count):
    return lax.ppermute(value, axis, [(i, i ^ distance) for i in range(count)])


def mul(first, second, dims=NN):
    return lax.dot_general(first, second, dims, preferred_element_type=F32)


def in_order(own, other, index, axis):
    return jnp.where(
        index == 0,
        jnp.concatenate([own, other], axis=axis),
        jnp.concatenate([other, own], axis=axis),
    )


def my_half(value, wt):
    half = value.shape[1] // 2
    return jnp.where(wt == 0, value[:, :half], value[:, half:])


def turned(value):
    return value.astype(F32).T.astype(BF)


def store_rows(out, full, owner, last):
    piece = full.shape[0] // 4
    for j in range(4):
        base = owner if j % 2 == 0 else last - owner
        start = pl.multiple_of(base * (2 * piece) + (j // 2) * piece, piece)
        out[pl.ds(start, piece), :] = full[j * piece : (j + 1) * piece]


def own_rows(ref, ctx, last, tok_rows):
    piece = tok_rows // 4
    parts = []
    for j in range(4):
        base = ctx if j % 2 == 0 else last - ctx
        start = pl.multiple_of(base * (2 * piece) + (j // 2) * piece, piece)
        parts.append(ref[pl.ds(start, piece), :])
    return jnp.concatenate(parts, axis=0)


def rotated(first, second, cosines, sines, sign):
    return first * cosines - sign * second * sines, second * cosines + sign * first * sines


def norm_scale(value):
    return lax.rsqrt(jnp.mean(value * value, axis=1, keepdims=True) + EPSILON)


def forward_kernel(
    where_ref,
    rows_ref,
    near_ref,
    across_ref,
    low_ref,
    high_ref,
    proj_ref,
    first_ref,
    second_ref,
    gain_ref,
    other_gain_ref,
    cos_ref,
    sin_ref,
    x_ref,
    h1_ref,
    q_ref,
    k_ref,
    v_ref,
    o_ref,
    lse_ref,
    resid_ref,
    h2_ref,
    h2t_ref,
    weights_ref,
    h1t_ref,
    other_ref,
):
    ctx, wt, seq = where_ref[0], where_ref[1], where_ref[2]
    count, tok_rows, part_width = rows_ref.shape
    last = 4 * count - 1
    rows = x_ref.shape[0]
    query_width = QUERY_HEADS * HEAD_SIZE
    pair_width = KEY_VALUE_HEADS * HEAD_SIZE
    half_dim = HEAD_SIZE // 2
    for k in range(count):
        for d in range(2):
            own = rows_ref[k] if d == 0 else near_ref[k]
            if d == 0:
                other = across_ref[k]
            else:
                other = low_ref[k] if k < count // 2 else high_ref[k - count // 2]
            owner = jnp.bitwise_xor(ctx, ROW_DISTANCES[k] + d)
            store_rows(x_ref, in_order(own, other, wt, 1), owner, last)
    half = first_ref.shape[0]
    other_ref[pl.ds(pl.multiple_of(seq * half, 16), half), :] = first_ref[...]
    other_ref[pl.ds(pl.multiple_of((1 - seq) * half, 16), half), :] = second_ref[...]
    weights_ref[...] = in_order(proj_ref[...], other_ref[...], wt, 1)
    gains = in_order(gain_ref[...], other_gain_ref[...], wt, 1)
    x = x_ref[...].astype(F32)
    hidden_one = x * norm_scale(x) * gains[0:1]
    h1t_ref[...] = hidden_one.T.astype(BF)
    h1_ref[...] = h1t_ref[pl.ds(pl.multiple_of(wt * part_width, 16), part_width), :]
    cosines, sines = cos_ref[...], sin_ref[...]
    heads = QUERY_HEADS + 2 * KEY_VALUE_HEADS
    for head in range(heads):
        at = head * HEAD_SIZE
        value = mul(weights_ref[at : at + HEAD_SIZE], h1t_ref[...])
        if at < query_width + pair_width:
            low, high = rotated(value[:half_dim], value[half_dim:], cosines, sines, 1.0)
            value = jnp.concatenate([low, high], axis=0)
        if at < query_width:
            q_ref[at : at + HEAD_SIZE] = value.astype(BF) * BF(0.125)
        elif at < query_width + pair_width:
            at -= query_width
            k_ref[at : at + HEAD_SIZE] = value.astype(BF)
        else:
            at -= query_width + pair_width
            v_ref[at : at + HEAD_SIZE] = value.astype(BF)

    repeat = QUERY_HEADS // KEY_VALUE_HEADS
    tile = min(FORWARD_TILE, rows)
    causal = lax.broadcasted_iota(jnp.int32, (tile, tile), 0) <= lax.broadcasted_iota(
        jnp.int32, (tile, tile), 1
    )

    def group(g, carry):
        pair_at = pl.ds(pl.multiple_of(g * HEAD_SIZE, HEAD_SIZE), HEAD_SIZE)
        keys = turned(k_ref[pair_at, :])
        values = jnp.concatenate([v_ref[pair_at, :], jnp.ones((16, rows), BF)], axis=0)
        for r in range(repeat):
            head = g * repeat + r
            head_at = pl.ds(pl.multiple_of(head * HEAD_SIZE, HEAD_SIZE), HEAD_SIZE)
            for start in range(0, rows, tile):
                stop = start + tile
                query = q_ref[head_at, start:stop]
                scores = jnp.where(causal, mul(keys[start:stop], query), -1e30)
                top = jnp.max(scores, axis=0, keepdims=True)
                if start:
                    before = mul(keys[:start], query)
                    top = jnp.maximum(top, jnp.max(before, axis=0, keepdims=True))
                weights = jnp.exp(scores - top).astype(BF)
                out = mul(values[:, start:stop], weights)
                if start:
                    out += mul(values[:, :start], jnp.exp(before - top).astype(BF))
                total = out[HEAD_SIZE : HEAD_SIZE + 1]
                o_ref[head_at, start:stop] = (out[:HEAD_SIZE] / total).astype(BF)
                lse_ref[head, :, start:stop] = top + jnp.log(total)
        return carry

    lax.fori_loop(0, KEY_VALUE_HEADS, group, 0)
    out_weights = weights_ref[query_width + 2 * pair_width :]
    resid = x_ref[...].astype(F32) + mul(o_ref[...], out_weights, TN)
    resid_ref[...] = resid
    hidden_two = resid * norm_scale(resid) * gains[1:2]
    h2_ref[...] = hidden_two.astype(BF)
    h2t_ref[...] = hidden_two.T.astype(BF)


def mlp_chunk(hidden_two, cots, gate, up, down):
    gate_pre = mul(hidden_two, gate, NT)
    up_pre = mul(hidden_two, up, NT)
    act_grad = mul(cots, down, NT)
    sigmoid_gate = jax.nn.sigmoid(gate_pre)
    silu = gate_pre * sigmoid_gate
    activated = (silu * up_pre).astype(BF)
    gate_grad = (act_grad * up_pre * (sigmoid_gate + silu * (1.0 - sigmoid_gate))).astype(BF)
    up_grad = (act_grad * silu).astype(BF)
    back = mul(gate_grad, gate) + mul(up_grad, up)
    return activated, gate_grad, up_grad, back


def own_mlp_kernel(
    where_ref,
    pairs_ref,
    far_ref,
    h2_ref,
    h2t_ref,
    w_ref,
    cot_ref,
    grads_ref,
    grad_down_ref,
    back_ref,
    delta_ref,
    act_ref,
):
    ctx, wt = where_ref[0], where_ref[1]
    count, _, tok_rows, part_width = pairs_ref.shape
    last = 4 * count - 1
    for k in range(2 * count):
        ref = pairs_ref if k < count else far_ref
        full = in_order(ref[k % count, 0], ref[k % count, 1], wt, 1)
        store_rows(cot_ref, full, jnp.bitwise_xor(ctx, k), last)
    hidden = w_ref.shape[1]
    tile = HIDDEN_TILE
    back_ref[...] = jnp.zeros_like(back_ref)
    delta_ref[...] = jnp.zeros_like(delta_ref)

    def chunk(j, carry):
        at = pl.ds(pl.multiple_of(j * tile, tile), tile)
        down = w_ref[2, at, :]
        activated, gate_grad, up_grad, back = mlp_chunk(
            h2_ref[...], cot_ref[...], w_ref[0, at, :], w_ref[1, at, :], down
        )
        back_ref[...] += back
        act_ref[...] = activated
        delta_ref[...] += mul(own_rows(act_ref, ctx, last, tok_rows), down)
        grads_ref[0, :, at] = mul(h2t_ref[...], gate_grad).astype(BF)
        grads_ref[1, :, at] = mul(h2t_ref[...], up_grad).astype(BF)
        grad_down_ref[at, :] = mul(activated, cot_ref[...], TN).astype(BF)
        return carry

    lax.fori_loop(0, hidden // tile, chunk, 0)


def other_mlp_kernel(
    where_ref,
    h2_ref,
    cot_ref,
    first_ref,
    second_ref,
    back_in_ref,
    delta_in_ref,
    resid_ref,
    gain_ref,
    other_gain_ref,
    o_ref,
    out_ref,
    mid_ref,
    mid_bf_ref,
    grad_out_ref,
    w_ref,
    act_ref,
    back_ref,
    delta_ref,
):
    ctx, wt = where_ref[0], where_ref[1]
    rows = h2_ref.shape[0]
    tok_rows, part_width = out_ref.shape
    last = 2 * rows // tok_rows - 1
    half = first_ref.shape[1]
    w_ref[:, :half] = first_ref[...]
    w_ref[:, half:] = second_ref[...]
    tile = HIDDEN_TILE
    back_ref[...] = back_in_ref[...]
    delta_ref[...] = delta_in_ref[...]

    def chunk(j, carry):
        at = pl.ds(pl.multiple_of(j * tile, tile), tile)
        down = w_ref[2, at, :]
        activated, _, _, back = mlp_chunk(
            h2_ref[...], cot_ref[...], w_ref[0, at, :], w_ref[1, at, :], down
        )
        back_ref[...] += back
        act_ref[...] = activated
        delta_ref[...] += mul(own_rows(act_ref, ctx, last, tok_rows), down)
        return carry

    lax.fori_loop(0, 2 * half // tile, chunk, 0)
    gains = in_order(gain_ref[...], other_gain_ref[...], wt, 1)
    layer_out = own_rows(resid_ref, ctx, last, tok_rows) + delta_ref[...]
    out_ref[...] = my_half(layer_out, wt).astype(BF)
    resid = resid_ref[...]
    scale = norm_scale(resid)
    normed = resid * scale
    back = back_ref[...]
    gain_grad = jnp.sum(back * normed, axis=0, keepdims=True)
    scaled = back * gains[1:2]
    mean = jnp.mean(scaled * normed, axis=1, keepdims=True)
    mid = cot_ref[...].astype(F32) + scale * (scaled - normed * mean)
    mid_ref[...] = mid
    mid_bf = mid.astype(BF)
    mid_bf_ref[...] = mid_bf
    height = o_ref.shape[0]
    grad_out_ref[:height] = mul(o_ref[...], my_half(mid_bf, wt)).astype(BF)
    gain_rows = jnp.broadcast_to(my_half(gain_grad, wt), (16, part_width))
    grad_out_ref[height:] = gain_rows.astype(BF)


def backward_kernel(
    weights_ref,
    mid_bf_ref,
    q_ref,
    k_ref,
    v_ref,
    o_ref,
    lse_ref,
    cos_ref,
    sin_ref,
    h1_ref,
    own_ref,
    got_ref,
    own_down_ref,
    got_down_ref,
    proj_ref,
    grad_ref,
    gate_out,
    up_out,
    down_out,
    g_ref,
    dk_ref,
    dv_ref,
    sum_ref,
    sum_down_ref,
    sems,
):
    rows = q_ref.shape[1]
    query_width = QUERY_HEADS * HEAD_SIZE
    pair_width = KEY_VALUE_HEADS * HEAD_SIZE
    half_dim = HEAD_SIZE // 2
    for i in range(2):
        sum_ref[i] = own_ref[i].astype(F32) + got_ref[i].astype(F32)
    sum_down_ref[...] = own_down_ref[...].astype(F32) + got_down_ref[...].astype(F32)
    copies = [
        pltpu.make_async_copy(sum_ref.at[0], gate_out, sems.at[0]),
        pltpu.make_async_copy(sum_ref.at[1], up_out, sems.at[1]),
        pltpu.make_async_copy(sum_down_ref, down_out, sems.at[2]),
    ]
    for copy in copies:
        copy.start()
    g_ref[...] = mul(weights_ref[query_width + 2 * pair_width :], mid_bf_ref[...], NT).astype(BF)
    repeat = QUERY_HEADS // KEY_VALUE_HEADS
    tile = min(BACKWARD_TILE, rows)
    causal = lax.broadcasted_iota(jnp.int32, (tile, tile), 0) <= lax.broadcasted_iota(
        jnp.int32, (tile, tile), 1
    )

    def unturn(value, start, stop):
        cosines, sines = cos_ref[:, start:stop], sin_ref[:, start:stop]
        low, high = rotated(value[:half_dim], value[half_dim:], cosines, sines, -1.0)
        return jnp.concatenate([low, high], axis=0).astype(BF)

    def group(g, carry):
        pair_at = pl.ds(pl.multiple_of(g * HEAD_SIZE, HEAD_SIZE), HEAD_SIZE)
        keys_t = k_ref[pair_at, :]
        keys, values = turned(keys_t), turned(v_ref[pair_at, :])
        dk_ref[...] = jnp.zeros_like(dk_ref)
        dv_ref[...] = jnp.zeros_like(dv_ref)
        for r in range(repeat):
            head = g * repeat + r
            head_at = pl.ds(pl.multiple_of(head * HEAD_SIZE, HEAD_SIZE), HEAD_SIZE)
            product = g_ref[head_at, :].astype(F32) * o_ref[head_at, :].astype(F32)
            delta = jnp.sum(product, axis=0, keepdims=True)
            for start in range(0, rows, tile):
                stop = start + tile
                query, grad = q_ref[head_at, start:stop], g_ref[head_at, start:stop]
                lse = lse_ref[head, :, start:stop]
                scores = mul(keys[:stop], query)
                prob_grad = mul(values[:stop], grad)
                probs = jnp.where(causal, jnp.exp(scores[start:] - lse), 0.0)
                if start:
                    probs = jnp.concatenate([jnp.exp(scores[:start] - lse), probs], axis=0)
                score_grad = (probs * (prob_grad - delta[:, start:stop])).astype(BF)
                probs = probs.astype(BF)
                dq = mul(keys_t[:, :stop], score_grad) * 0.125
                proj_ref[head_at, start:stop] = unturn(dq, start, stop)
                dk_ref[:, :stop] += mul(query, score_grad, NT)
                dv_ref[:, :stop] += mul(grad, probs, NT)
        key_at = pl.multiple_of(query_width + g * HEAD_SIZE, HEAD_SIZE)
        proj_ref[pl.ds(key_at, HEAD_SIZE), :] = unturn(dk_ref[...], 0, rows)
        value_at = pl.multiple_of(query_width + pair_width + g * HEAD_SIZE, HEAD_SIZE)
        proj_ref[pl.ds(value_at, HEAD_SIZE), :] = dv_ref[...].astype(BF)
        return carry

    lax.fori_loop(0, KEY_VALUE_HEADS, group, 0)
    grad_ref[...] = mul(h1_ref[...], proj_ref[...], NT).astype(BF)
    for copy in copies:
        copy.wait()


def input_kernel(
    where_ref, proj_ref, weights_ref, x_ref, mid_ref, gain_ref, other_gain_ref, out_ref
):
    ctx, wt = where_ref[0], where_ref[1]
    rows = proj_ref.shape[1]
    tok_rows, part_width = out_ref.shape
    last = 2 * rows // tok_rows - 1
    piece = tok_rows // 4
    at = lax.broadcasted_iota(jnp.int32, (rows, tok_rows), 0)
    u = lax.broadcasted_iota(jnp.int32, (rows, tok_rows), 1)
    j = u // piece
    base = jnp.where(j % 2 == 0, ctx, last - ctx)
    position = base * (2 * piece) + (j // 2) * piece + u % piece
    chosen = jnp.where(at == position, 1.0, 0.0).astype(BF)
    mine = mul(proj_ref[...], chosen).astype(BF)
    grad = mul(mine, weights_ref[: proj_ref.shape[0]], TN)
    gains = in_order(gain_ref[...], other_gain_ref[...], wt, 1)
    x = own_rows(x_ref, ctx, last, tok_rows).astype(F32)
    mid = own_rows(mid_ref, ctx, last, tok_rows)
    scale = norm_scale(x)
    normed = x * scale
    scaled = grad * gains[0:1]
    mean = jnp.mean(scaled * normed, axis=1, keepdims=True)
    out_ref[...] = my_half(mid + scale * (scaled - normed * mean), wt)


def whole_device(layer_input, cotangent, w_qkv, w_out, w_gate, w_up, w_down, gain_attn, gain_mlp):
    ctx_count = lax.axis_size("ctx")
    ctx_index = lax.axis_index("ctx")
    wt_index = lax.axis_index("wt")
    seq_index = lax.axis_index("seq")
    where = jnp.stack([ctx_index, wt_index, seq_index]).astype(jnp.int32)
    tok_rows, part_width = layer_input.shape[1:]
    full_width = 2 * part_width
    rows = tok_rows * ctx_count
    query_width = QUERY_HEADS * HEAD_SIZE
    pair_width = KEY_VALUE_HEADS * HEAD_SIZE
    proj_width = query_width + 2 * pair_width
    hidden = w_gate.shape[1]
    shape = jax.ShapeDtypeStruct

    def across_ctx(value, distance):
        return swap(value, "ctx", distance, ctx_count)

    def half_of(value, axis):
        half = value.shape[axis] // 2
        return lax.dynamic_slice_in_dim(value, seq_index * half, half, axis)

    block = layer_input[0]
    row_blocks = block[None]
    for distance in (4, 2):
        row_blocks = jnp.concatenate([row_blocks, across_ctx(row_blocks, distance)], axis=0)
    near = across_ctx(row_blocks, 1)
    across = swap(row_blocks, "wt", 1, 2)
    low = swap(near[:2], "wt", 1, 2)
    high = across_ctx(across[2:], 1)

    projections = jnp.concatenate([w_qkv.T, w_out], axis=0)
    first = swap(half_of(projections, 0), "wt", 1, 2)
    second = swap(first, "seq", 1, 2)
    gains = jnp.stack([gain_attn, gain_mlp])
    other_gains = swap(gains, "wt", 1, 2)

    cot = cotangent[0][None]
    cot = jnp.concatenate([cot, swap(cot, "wt", 1, 2)], axis=0)[None]
    for distance in (1, 2):
        cot = jnp.concatenate([cot, across_ctx(cot, distance)], axis=0)
    cot_far = across_ctx(cot, 4)

    mlp = jnp.stack([w_gate.T, w_up.T, w_down])
    mlp_half, low, high = lax.optimization_barrier((half_of(mlp, 1), low, high))
    mlp_first = swap(mlp_half, "wt", 1, 2)
    mlp_second = swap(mlp_first, "seq", 1, 2)

    half_dim = HEAD_SIZE // 2
    frequency = jnp.power(F32(ROPE_BASE), -jnp.arange(half_dim, dtype=F32) * 2.0 / HEAD_SIZE)
    angles = frequency[:, None] * jnp.arange(rows, dtype=F32)[None, :]
    cosines, sines = jnp.cos(angles), jnp.sin(angles)

    x, h1_t, q_t, k_t, v_t, o_t, lse, resid, h2, h2_t, weights = pl.pallas_call(
        forward_kernel,
        in_specs=[SMEM] + [VMEM] * 12,
        out_specs=[VMEM] * 11,
        out_shape=[
            shape((rows, full_width), BF),
            shape((part_width, rows), BF),
            shape((query_width, rows), BF),
            shape((pair_width, rows), BF),
            shape((pair_width, rows), BF),
            shape((query_width, rows), BF),
            shape((QUERY_HEADS, 1, rows), F32),
            shape((rows, full_width), F32),
            shape((rows, full_width), BF),
            shape((full_width, rows), BF),
            shape((proj_width + query_width, full_width), BF),
        ],
        scratch_shapes=[
            pltpu.VMEM((full_width, rows), BF),
            pltpu.VMEM((proj_width + query_width, part_width), BF),
        ],
        name="forward",
    )(
        where, row_blocks, near, across, low, high,
        projections, first, second, gains, other_gains, cosines, sines,
    )

    cots, grads, grad_down, back, delta = pl.pallas_call(
        own_mlp_kernel,
        in_specs=[SMEM] + [VMEM] * 5,
        out_specs=[VMEM] * 5,
        out_shape=[
            shape((rows, full_width), BF),
            shape((2, full_width, hidden), BF),
            shape((hidden, full_width), BF),
            shape((rows, full_width), F32),
            shape((tok_rows, full_width), F32),
        ],
        scratch_shapes=[pltpu.VMEM((rows, HIDDEN_TILE), BF)],
        name="own_mlp",
    )(where, cot, cot_far, h2, h2_t, mlp)
    got = swap(grads, "seq", 1, 2)
    got_down = swap(grad_down, "seq", 1, 2)

    layer_out, mid, mid_bf, grad_out = pl.pallas_call(
        other_mlp_kernel,
        in_specs=[SMEM] + [VMEM] * 10,
        out_specs=[VMEM] * 4,
        out_shape=[
            shape((tok_rows, part_width), BF),
            shape((rows, full_width), F32),
            shape((rows, full_width), BF),
            shape((query_width + 16, part_width), BF),
        ],
        scratch_shapes=[
            pltpu.VMEM((3, hidden, full_width), BF),
            pltpu.VMEM((rows, HIDDEN_TILE), BF),
            pltpu.VMEM((rows, full_width), F32),
            pltpu.VMEM((tok_rows, full_width), F32),
        ],
        name="other_mlp",
    )(where, h2, cots, mlp_first, mlp_second, back, delta, resid, gains, other_gains, o_t)
    got_out = swap(grad_out, "seq", 1, 2)

    proj_t, grad_qkv, grad_gate, grad_up, grad_down = pl.pallas_call(
        backward_kernel,
        in_specs=[VMEM] * 14,
        out_specs=[VMEM] * 2 + [ANY] * 3,
        out_shape=[
            shape((proj_width, rows), BF),
            shape((part_width, proj_width), BF),
            shape((full_width, hidden), F32),
            shape((full_width, hidden), F32),
            shape((hidden, full_width), F32),
        ],
        scratch_shapes=[
            pltpu.VMEM((query_width, rows), BF),
            pltpu.VMEM((HEAD_SIZE, rows), F32),
            pltpu.VMEM((HEAD_SIZE, rows), F32),
            pltpu.VMEM((2, full_width, hidden), F32),
            pltpu.VMEM((hidden, full_width), F32),
            pltpu.SemaphoreType.DMA((3,)),
        ],
        name="backward",
    )(
        weights, mid_bf, q_t, k_t, v_t, o_t, lse, cosines, sines, h1_t,
        grads, got, grad_down, got_down,
    )
    got_qkv = swap(grad_qkv, "seq", 1, 2)
    input_grad = pl.pallas_call(
        input_kernel,
        in_specs=[SMEM] + [VMEM] * 6,
        out_specs=VMEM,
        out_shape=shape((tok_rows, part_width), F32),
        name="input_grad",
    )(where, proj_t, weights, x, mid, gains, other_gains)

    out_sum = grad_out.astype(F32) + got_out.astype(F32)
    qkv_sum = grad_qkv.astype(F32) + got_qkv.astype(F32)
    grad_gain_attn = jnp.sum(qkv_sum * w_qkv.astype(F32), axis=1) / gain_attn
    return (
        layer_out[None],
        input_grad[None],
        qkv_sum,
        out_sum[:query_width],
        grad_gate,
        grad_up,
        grad_down,
        grad_gain_attn,
        out_sum[query_width],
    )


def solution(mesh):
    in_specs = (
        P("seq", "ctx", "wt"),
        P("seq", "ctx", "wt"),
        P("wt", None),
        P(None, "wt"),
        P(None, "wt"),
        P(None, "wt"),
        P("wt", None),
        P("wt"),
        P("wt"),
    )
    out_specs = (
        P("seq", "ctx", "wt"),
        P("seq", "ctx", "wt"),
        P("wt", None),
        P(None, "wt"),
        P(None, "wt"),
        P(None, "wt"),
        P("wt", None),
        P("wt"),
        P("wt"),
    )
    sizes = mesh.shape
    whole = sizes["wt"] == 2 and sizes["seq"] == 2 and sizes["ctx"] == 8
    return jax.shard_map(
        whole_device if whole else split_device, mesh=mesh, in_specs=in_specs, out_specs=out_specs, check_vma=False
    )
```

```python
import jax
import jax.numpy as jnp
from jax import lax
from jax.experimental import pallas as pl
from jax.experimental.pallas import tpu as pltpu
from jax.sharding import PartitionSpec as P

QUERY_HEADS = 9
KEY_VALUE_HEADS = 3
HEAD_SIZE = 64


EPSILON = 1e-05
ROPE_BASE = 100000.0


def row_sums(partial_value):
    return lax.psum(partial_value, "wt")


def rope_tables(positions):
    half_dim = HEAD_SIZE // 2
    frequency = jnp.power(
        jnp.float32(ROPE_BASE), -jnp.arange(half_dim, dtype=jnp.float32) * 2.0 / HEAD_SIZE
    )
    angles = positions.astype(jnp.float32)[:, None] * frequency[None, :]
    angles = jnp.concatenate([angles, angles], axis=1)
    return (jnp.cos(angles), jnp.sin(angles))


def rotate(tensor):
    half_dim = tensor.shape[-1] // 2
    return jnp.concatenate([-tensor[..., half_dim:], tensor[..., :half_dim]], axis=-1)


def apply_rotation(tensor, cosine_values, sine_values):
    return tensor * cosine_values[:, None, :] + rotate(tensor) * sine_values[:, None, :]


def reverse_rotation(tensor, cosine_values, sine_values):
    return tensor * cosine_values[:, None, :] - rotate(tensor) * sine_values[:, None, :]


def select_group(values_in, group_index):
    return lax.dynamic_index_in_dim(values_in, group_index, 0, keepdims=False)


def fetch_block(kv_stack, source, row_start, key_tile):
    key_value_half = kv_stack.shape[2] // 2
    key_value_block = lax.dynamic_slice(
        kv_stack, (source, row_start, 0), (1, key_tile, kv_stack.shape[2])
    )[0]
    key_portion = key_value_block[:, :key_value_half].reshape(key_tile, KEY_VALUE_HEADS, HEAD_SIZE)
    value_portion = key_value_block[:, key_value_half:].reshape(
        key_tile, KEY_VALUE_HEADS, HEAD_SIZE
    )
    return (key_portion, value_portion)


def split_device(layer_input, cotangent, w_qkv, w_out, w_gate, w_up, w_down, gain_attn, gain_mlp):
    ctx_count = lax.axis_size("ctx")
    wt_count = lax.axis_size("wt")
    ctx_index = lax.axis_index("ctx")
    wt_index = lax.axis_index("wt")
    resid_in = layer_input[0].astype(jnp.float32)
    tok_rows, part_width = resid_in.shape
    full_width = part_width * wt_count
    local_rows = tok_rows // wt_count
    segment_rows = local_rows // 2
    block_rows = tok_rows // 2
    repeat_factor = QUERY_HEADS // KEY_VALUE_HEADS
    query_total_width = QUERY_HEADS * HEAD_SIZE
    key_value_width = KEY_VALUE_HEADS * HEAD_SIZE
    scale_one = lax.rsqrt(row_sums(jnp.sum(resid_in * resid_in, axis=1)) / full_width + EPSILON)[
        :, None
    ]
    normed_one = resid_in * scale_one
    hidden_one = (normed_one * gain_attn).astype(jnp.bfloat16)
    rows_in = hidden_one
    projected_rows = lax.psum_scatter(
        jnp.dot(rows_in, w_qkv, preferred_element_type=jnp.float32).astype(jnp.bfloat16),
        "wt",
        scatter_dimension=0,
        tiled=True,
    ).astype(jnp.float32)
    offsets = jnp.arange(segment_rows, dtype=jnp.int32)
    early_pos = ctx_index * block_rows + wt_index * segment_rows + offsets
    late_pos = (2 * ctx_count - 1 - ctx_index) * block_rows + wt_index * segment_rows + offsets
    query_pos = jnp.stack([early_pos, late_pos])
    cosine_values, sine_values = rope_tables(query_pos.reshape(local_rows))
    query_rows = apply_rotation(
        projected_rows[:, :query_total_width].reshape(local_rows, QUERY_HEADS, HEAD_SIZE),
        cosine_values,
        sine_values,
    )
    query_rows = query_rows.astype(jnp.bfloat16).reshape(
        2, segment_rows, KEY_VALUE_HEADS, repeat_factor, HEAD_SIZE
    )
    key_row_slice = apply_rotation(
        projected_rows[:, query_total_width : query_total_width + key_value_width].reshape(
            local_rows, KEY_VALUE_HEADS, HEAD_SIZE
        ),
        cosine_values,
        sine_values,
    )
    key_row_slice = key_row_slice.astype(jnp.bfloat16).reshape(local_rows, key_value_width)
    value_row_slice = projected_rows[:, query_total_width + key_value_width :].astype(jnp.bfloat16)
    kv_pair = jnp.concatenate([key_row_slice, value_row_slice], axis=1).reshape(
        2, segment_rows, 2 * key_value_width
    )
    kv_all = lax.all_gather(kv_pair, ("ctx", "wt"), axis=1, tiled=True)
    half_len = kv_all.shape[1]
    key_tile = min(1024, half_len)
    block_total = half_len // key_tile
    early_count = (ctx_index * block_rows + (wt_index + 1) * segment_rows - 1) // key_tile + 1
    late_count = (
        (ctx_count - 1 - ctx_index) * block_rows + (wt_index + 1) * segment_rows - 1
    ) // key_tile + 1
    turn_total = early_count + block_total + late_count

    def locate(turn_index):
        query_group = (turn_index >= early_count).astype(jnp.int32)
        late_turn = turn_index - early_count
        source = query_group * (late_turn >= block_total).astype(jnp.int32)
        block_index = jnp.where(
            query_group == 0,
            turn_index,
            jnp.where(source == 0, late_turn, 2 * block_total - 1 - late_turn),
        )
        row_start = block_index * key_tile
        key_index = row_start + jnp.arange(key_tile, dtype=jnp.int32)
        late_keys = (
            2 * ctx_count - 1 - key_index // block_rows
        ) * block_rows + key_index % block_rows
        key_pos = jnp.where(source == 0, key_index, late_keys)
        return (query_group, source, row_start, key_pos)

    def group_scores(kv_stack, turn_index):
        query_group, source, row_start, key_pos = locate(turn_index)
        key_portion, value_portion = fetch_block(kv_stack, source, row_start, key_tile)
        query_sel = select_group(query_rows, query_group)
        scores = (
            jnp.einsum("pgrd,kgd->pgrk", query_sel, key_portion, preferred_element_type=jnp.float32)
            * 0.125
        )
        key_mask = (key_pos[None, :] <= select_group(query_pos, query_group)[:, None])[
            :, None, None, :
        ]
        scores = jnp.where(key_mask, scores, -1e30)
        return (
            query_group,
            source,
            row_start,
            query_sel,
            key_portion,
            value_portion,
            scores,
            key_mask,
        )

    def forward_turn(turn_index, loop_state):
        running_max, running_sum, attended_acc = loop_state
        query_group, source, row_start, query_sel, key_portion, value_portion, scores, key_mask = (
            group_scores(kv_all, turn_index)
        )
        previous = select_group(running_max, query_group)
        updated = jnp.maximum(previous, jnp.max(scores, axis=-1))
        shrink = jnp.exp(previous - updated)
        weights = jnp.where(key_mask, jnp.exp(scores - updated[..., None]), 0.0)
        summed_exp = select_group(running_sum, query_group) * shrink + jnp.sum(weights, axis=-1)
        gained = select_group(attended_acc, query_group) * shrink[..., None] + jnp.einsum(
            "pgrk,kgd->pgrd",
            weights.astype(jnp.bfloat16),
            value_portion,
            preferred_element_type=jnp.float32,
        )
        return (
            lax.dynamic_update_index_in_dim(running_max, updated, query_group, 0),
            lax.dynamic_update_index_in_dim(running_sum, summed_exp, query_group, 0),
            lax.dynamic_update_index_in_dim(attended_acc, gained, query_group, 0),
        )

    statistic_shape = (2, segment_rows, KEY_VALUE_HEADS, repeat_factor)
    running_max, running_sum, attended_acc = lax.fori_loop(
        0,
        turn_total,
        forward_turn,
        (
            jnp.full(statistic_shape, -1e30, jnp.float32),
            jnp.zeros(statistic_shape, jnp.float32),
            jnp.zeros((2, segment_rows, KEY_VALUE_HEADS, repeat_factor, HEAD_SIZE), jnp.float32),
        ),
    )
    logsumexp_every = running_max + jnp.log(running_sum)
    attended_rows = (attended_acc / running_sum[..., None]).astype(jnp.bfloat16)
    attended_all = lax.all_gather(
        attended_rows.reshape(local_rows, query_total_width), "wt", axis=0, tiled=True
    )
    resid_mid = resid_in + jnp.dot(attended_all, w_out, preferred_element_type=jnp.float32)
    scale_two = lax.rsqrt(row_sums(jnp.sum(resid_mid * resid_mid, axis=1)) / full_width + EPSILON)[
        :, None
    ]
    normed_two = resid_mid * scale_two
    hidden_two = (normed_two * gain_mlp).astype(jnp.bfloat16)
    hidden_full = lax.all_gather(hidden_two, "wt", axis=1, tiled=True)
    gate_pre = jnp.dot(hidden_full, w_gate, preferred_element_type=jnp.float32)
    up_pre = jnp.dot(hidden_full, w_up, preferred_element_type=jnp.float32)
    sigmoid_gate = jax.nn.sigmoid(gate_pre)
    activated = (gate_pre * sigmoid_gate * up_pre).astype(jnp.bfloat16)
    down_terms = jnp.dot(activated, w_down, preferred_element_type=jnp.float32)
    mlp_delta = lax.psum_scatter(
        down_terms.astype(jnp.bfloat16), "wt", scatter_dimension=1, tiled=True
    ).astype(jnp.float32)
    layer_out = (resid_mid + mlp_delta).astype(jnp.bfloat16)
    cot_rows = cotangent[0]
    cot_full = lax.all_gather(cot_rows, "wt", axis=1, tiled=True)
    act_grad = jnp.dot(cot_full, w_down.T, preferred_element_type=jnp.float32)
    gate_grad = (act_grad * up_pre * sigmoid_gate * (1.0 + gate_pre * (1.0 - sigmoid_gate))).astype(
        jnp.bfloat16
    )
    up_grad = (act_grad * gate_pre * sigmoid_gate).astype(jnp.bfloat16)
    grad_down = jnp.dot(activated.T, cot_full, preferred_element_type=jnp.float32)
    grad_gate = jnp.dot(hidden_full.T, gate_grad, preferred_element_type=jnp.float32)
    grad_up = jnp.dot(hidden_full.T, up_grad, preferred_element_type=jnp.float32)
    hidden_terms = jnp.dot(gate_grad, w_gate.T, preferred_element_type=jnp.float32) + jnp.dot(
        up_grad, w_up.T, preferred_element_type=jnp.float32
    )
    hidden_two_grad = lax.psum_scatter(
        hidden_terms.astype(jnp.bfloat16), "wt", scatter_dimension=1, tiled=True
    ).astype(jnp.float32)
    grad_gain_mlp = jnp.sum(hidden_two_grad * normed_two, axis=0)
    norm_two_grad = hidden_two_grad * gain_mlp
    mean_two = row_sums(jnp.sum(norm_two_grad * normed_two, axis=1)) / full_width
    mid_grad = cot_rows.astype(jnp.float32) + scale_two * (
        norm_two_grad - normed_two * mean_two[:, None]
    )
    mid_rounded = mid_grad.astype(jnp.bfloat16)
    grad_out = jnp.dot(attended_all.T, mid_rounded, preferred_element_type=jnp.float32)
    rows_in = mid_rounded
    attended_gradient = lax.psum_scatter(
        jnp.dot(rows_in, w_out.T, preferred_element_type=jnp.float32).astype(jnp.bfloat16),
        "wt",
        scatter_dimension=0,
        tiled=True,
    )
    attended_gradient = attended_gradient.reshape(
        2, segment_rows, KEY_VALUE_HEADS, repeat_factor, HEAD_SIZE
    )
    row_delta = jnp.sum(
        attended_gradient.astype(jnp.float32) * attended_rows.astype(jnp.float32), axis=-1
    )
    kv_reused = lax.all_gather(kv_pair, ("ctx", "wt"), axis=1, tiled=True)

    def back_turn(turn_index, loop_state):
        query_acc, kv_acc = loop_state
        query_group, source, row_start, query_sel, key_portion, value_portion, scores, key_mask = (
            group_scores(kv_reused, turn_index)
        )
        grad_sel = select_group(attended_gradient, query_group)
        probs_full = jnp.exp(scores - select_group(logsumexp_every, query_group)[..., None])
        prob_grad = jnp.einsum(
            "pgrd,kgd->pgrk", grad_sel, value_portion, preferred_element_type=jnp.float32
        )
        score_grad = (
            probs_full * (prob_grad - select_group(row_delta, query_group)[..., None])
        ).astype(jnp.bfloat16)
        weight_bf = probs_full.astype(jnp.bfloat16)
        query_new = (
            select_group(query_acc, query_group)
            + jnp.einsum(
                "pgrk,kgd->pgrd", score_grad, key_portion, preferred_element_type=jnp.float32
            )
            * 0.125
        )
        key_part_grad = (
            jnp.einsum("pgrk,pgrd->kgd", score_grad, query_sel, preferred_element_type=jnp.float32)
            * 0.125
        )
        value_part_grad = jnp.einsum(
            "pgrk,pgrd->kgd", weight_bf, grad_sel, preferred_element_type=jnp.float32
        )
        update_rows = jnp.concatenate(
            [
                key_part_grad.reshape(key_tile, key_value_width),
                value_part_grad.reshape(key_tile, key_value_width),
            ],
            axis=1,
        )[None]
        previous = lax.dynamic_slice(kv_acc, (source, row_start, 0), update_rows.shape)
        kv_acc = lax.dynamic_update_slice(kv_acc, previous + update_rows, (source, row_start, 0))
        return (lax.dynamic_update_index_in_dim(query_acc, query_new, query_group, 0), kv_acc)

    query_acc, kv_acc = lax.fori_loop(
        0,
        turn_total,
        back_turn,
        (
            jnp.zeros((2, segment_rows, KEY_VALUE_HEADS, repeat_factor, HEAD_SIZE), jnp.float32),
            jnp.zeros((2, half_len, 2 * key_value_width), jnp.float32),
        ),
    )
    key_value_gradient = lax.psum_scatter(
        kv_acc, ("ctx", "wt"), scatter_dimension=1, tiled=True
    ).reshape(local_rows, 2 * key_value_width)
    query_gradient = reverse_rotation(
        query_acc.reshape(local_rows, QUERY_HEADS, HEAD_SIZE), cosine_values, sine_values
    )
    key_gradient = reverse_rotation(
        key_value_gradient[:, :key_value_width].reshape(local_rows, KEY_VALUE_HEADS, HEAD_SIZE),
        cosine_values,
        sine_values,
    )
    proj_grad = jnp.concatenate(
        [
            query_gradient.reshape(local_rows, query_total_width),
            key_gradient.reshape(local_rows, key_value_width),
            key_value_gradient[:, key_value_width:],
        ],
        axis=1,
    ).astype(jnp.bfloat16)
    proj_all = lax.all_gather(proj_grad, "wt", axis=0, tiled=True)
    grad_qkv = jnp.dot(hidden_one.T, proj_all, preferred_element_type=jnp.float32)
    hidden_one_grad = jnp.dot(proj_all, w_qkv.T, preferred_element_type=jnp.float32)
    grad_gain_attn = jnp.sum(hidden_one_grad * normed_one, axis=0)
    norm_one_grad = hidden_one_grad * gain_attn
    mean_one = row_sums(jnp.sum(norm_one_grad * normed_one, axis=1)) / full_width
    input_grad = mid_grad + scale_one * (norm_one_grad - normed_one * mean_one[:, None])
    summed = lax.psum(
        (grad_qkv, grad_out, grad_gate, grad_up, grad_down, grad_gain_attn, grad_gain_mlp),
        ("seq", "ctx"),
    )
    return (
        layer_out[None],
        input_grad[None],
        summed[0],
        summed[1],
        summed[2],
        summed[3],
        summed[4],
        summed[5],
        summed[6],
    )


FORWARD_TILE = 512
BACKWARD_TILE = 256
HIDDEN_TILE = 256
MIB = 1 << 20
NN = (((1,), (0,)), ((), ()))
NT = (((1,), (1,)), ((), ()))
TN = (((0,), (0,)), ((), ()))
BF = jnp.bfloat16
F32 = jnp.float32
VMEM = pl.BlockSpec(memory_space=pltpu.VMEM)
SMEM = pl.BlockSpec(memory_space=pltpu.SMEM)
ANY = pl.BlockSpec(memory_space=pl.ANY)


def swap(value, axis, distance, count):
    return lax.ppermute(value, axis, [(i, i ^ distance) for i in range(count)])


def mul(first, second, dims=NN):
    return lax.dot_general(first, second, dims, preferred_element_type=F32)


def in_order(own, other, index, axis):
    return jnp.where(
        index == 0,
        jnp.concatenate([own, other], axis=axis),
        jnp.concatenate([other, own], axis=axis),
    )


def my_half(value, wt):
    half = value.shape[1] // 2
    return jnp.where(wt == 0, value[:, :half], value[:, half:])


def turned(value):
    return value.astype(F32).T.astype(BF)


def store_rows(out, full, owner, last):
    piece = full.shape[0] // 4
    for j in range(4):
        base = owner if j % 2 == 0 else last - owner
        start = pl.multiple_of(base * (2 * piece) + (j // 2) * piece, piece)
        out[pl.ds(start, piece), :] = full[j * piece : (j + 1) * piece]


def own_rows(ref, ctx, last, tok_rows):
    piece = tok_rows // 4
    parts = []
    for j in range(4):
        base = ctx if j % 2 == 0 else last - ctx
        start = pl.multiple_of(base * (2 * piece) + (j // 2) * piece, piece)
        parts.append(ref[pl.ds(start, piece), :])
    return jnp.concatenate(parts, axis=0)


def rotated(first, second, cosines, sines, sign):
    return first * cosines - sign * second * sines, second * cosines + sign * first * sines


def norm_scale(value):
    return lax.rsqrt(jnp.mean(value * value, axis=1, keepdims=True) + EPSILON)


def forward_kernel(
    where_ref,
    one_ref,
    two_ref,
    near_one_ref,
    near_two_ref,
    across_one_ref,
    across_two_ref,
    low_ref,
    high_ref,
    proj_ref,
    first_ref,
    second_ref,
    out_ref,
    out_first_ref,
    out_second_ref,
    gain_ref,
    other_gain_ref,
    cos_ref,
    sin_ref,
    x_ref,
    h1_ref,
    q_ref,
    k_ref,
    v_ref,
    o_ref,
    lse_ref,
    resid_ref,
    h2_ref,
    h2t_ref,
    weights_ref,
    h1t_ref,
    flat_ref,
    flat_out_ref,
):
    ctx, wt, seq = where_ref[0], where_ref[1], where_ref[2]
    part_width = one_ref.shape[1]
    rows = x_ref.shape[0]
    last = 2 * rows // one_ref.shape[2] - 1
    query_width = QUERY_HEADS * HEAD_SIZE
    pair_width = KEY_VALUE_HEADS * HEAD_SIZE
    half_dim = HEAD_SIZE // 2
    sources = (
        (one_ref, across_one_ref, 0),
        (two_ref, across_two_ref, 2),
        (near_one_ref, low_ref, 1),
        (near_two_ref, high_ref, 3),
    )
    for own, other, distance in sources:
        for i in range(2):
            full = turned(in_order(own[i], other[i], wt, 0))
            store_rows(x_ref, full, jnp.bitwise_xor(ctx, distance + 4 * i), last)

    def assemble(out, own, first, second):
        half = first.shape[0]
        out[pl.ds(pl.multiple_of(wt * 2 * half, 16), 2 * half), :] = own[...]
        base = (1 - wt) * 2 * half
        out[pl.ds(pl.multiple_of(base + seq * half, 16), half), :] = first[...]
        out[pl.ds(pl.multiple_of(base + (1 - seq) * half, 16), half), :] = second[...]

    assemble(flat_ref, proj_ref, first_ref, second_ref)
    assemble(flat_out_ref, out_ref, out_first_ref, out_second_ref)
    weights_ref[: query_width + 2 * pair_width] = turned(flat_ref[...])
    weights_ref[query_width + 2 * pair_width :] = turned(flat_out_ref[...])
    gains = in_order(gain_ref[...], other_gain_ref[...], wt, 1)
    x = x_ref[...].astype(F32)
    hidden_one = x * norm_scale(x) * gains[0:1]
    h1t_ref[...] = hidden_one.T.astype(BF)
    h1_ref[...] = h1t_ref[pl.ds(pl.multiple_of(wt * part_width, 16), part_width), :]
    cosines, sines = cos_ref[...], sin_ref[...]
    heads = QUERY_HEADS + 2 * KEY_VALUE_HEADS
    for head in range(heads):
        at = head * HEAD_SIZE
        value = mul(weights_ref[at : at + HEAD_SIZE], h1t_ref[...])
        if at < query_width + pair_width:
            low, high = rotated(value[:half_dim], value[half_dim:], cosines, sines, 1.0)
            value = jnp.concatenate([low, high], axis=0)
        if at < query_width:
            q_ref[at : at + HEAD_SIZE] = value.astype(BF) * BF(0.125)
        elif at < query_width + pair_width:
            at -= query_width
            k_ref[at : at + HEAD_SIZE] = value.astype(BF)
        else:
            at -= query_width + pair_width
            v_ref[at : at + HEAD_SIZE] = value.astype(BF)

    repeat = QUERY_HEADS // KEY_VALUE_HEADS
    tile = min(FORWARD_TILE, rows)
    causal = lax.broadcasted_iota(jnp.int32, (tile, tile), 0) <= lax.broadcasted_iota(
        jnp.int32, (tile, tile), 1
    )

    def group(g, carry):
        pair_at = pl.ds(pl.multiple_of(g * HEAD_SIZE, HEAD_SIZE), HEAD_SIZE)
        keys = turned(k_ref[pair_at, :])
        values = jnp.concatenate([v_ref[pair_at, :], jnp.ones((16, rows), BF)], axis=0)
        for r in range(repeat):
            head = g * repeat + r
            head_at = pl.ds(pl.multiple_of(head * HEAD_SIZE, HEAD_SIZE), HEAD_SIZE)
            for start in range(0, rows, tile):
                stop = start + tile
                query = q_ref[head_at, start:stop]
                scores = jnp.where(causal, mul(keys[start:stop], query), -1e30)
                top = jnp.max(scores, axis=0, keepdims=True)
                if start:
                    before = mul(keys[:start], query)
                    top = jnp.maximum(top, jnp.max(before, axis=0, keepdims=True))
                weights = jnp.exp(scores - top).astype(BF)
                out = mul(values[:, start:stop], weights)
                if start:
                    out += mul(values[:, :start], jnp.exp(before - top).astype(BF))
                total = out[HEAD_SIZE : HEAD_SIZE + 1]
                o_ref[head_at, start:stop] = (out[:HEAD_SIZE] / total).astype(BF)
                lse_ref[head, :, start:stop] = top + jnp.log(total)
        return carry

    lax.fori_loop(0, KEY_VALUE_HEADS, group, 0)
    out_weights = weights_ref[query_width + 2 * pair_width :]
    resid = x_ref[...].astype(F32) + mul(o_ref[...], out_weights, TN)
    resid_ref[...] = resid
    hidden_two = resid * norm_scale(resid) * gains[1:2]
    h2_ref[...] = hidden_two.astype(BF)
    h2t_ref[...] = hidden_two.T.astype(BF)


def mlp_chunk(hidden_two, cots, gate, up, down):
    gate_pre = mul(hidden_two, gate)
    up_pre = mul(hidden_two, up)
    act_grad = mul(cots, down)
    sigmoid_gate = jax.nn.sigmoid(gate_pre)
    silu = gate_pre * sigmoid_gate
    activated = (silu * up_pre).astype(BF)
    gate_grad = (act_grad * up_pre * (sigmoid_gate + silu * (1.0 - sigmoid_gate))).astype(BF)
    up_grad = (act_grad * silu).astype(BF)
    back = mul(gate_grad, gate, NT) + mul(up_grad, up, NT)
    return activated, gate_grad, up_grad, back


def own_mlp_kernel(
    where_ref,
    pairs_ref,
    far_ref,
    h2_ref,
    h2t_ref,
    gate_ref,
    up_ref,
    down_ref,
    cot_ref,
    grads_ref,
    back_ref,
    delta_ref,
    act_ref,
    cott_ref,
):
    ctx, wt = where_ref[0], where_ref[1]
    count, _, part_width, tok_rows = pairs_ref.shape
    last = 4 * count - 1
    for k in range(2 * count):
        ref = pairs_ref if k < count else far_ref
        full = turned(in_order(ref[k % count, 0], ref[k % count, 1], wt, 0))
        store_rows(cot_ref, full, jnp.bitwise_xor(ctx, k), last)
    cott_ref[...] = turned(cot_ref[...])
    hidden = gate_ref.shape[1]
    tile = HIDDEN_TILE
    back_ref[...] = jnp.zeros_like(back_ref)
    delta_ref[...] = jnp.zeros_like(delta_ref)

    def chunk(j, carry):
        at = pl.ds(pl.multiple_of(j * tile, tile), tile)
        down = down_ref[:, at]
        activated, gate_grad, up_grad, back = mlp_chunk(
            h2_ref[...], cot_ref[...], gate_ref[:, at], up_ref[:, at], down
        )
        back_ref[...] += back
        act_ref[...] = activated
        delta_ref[...] += mul(own_rows(act_ref, ctx, last, tok_rows), down, NT)
        grads_ref[0, :, at] = mul(h2t_ref[...], gate_grad).astype(BF)
        grads_ref[1, :, at] = mul(h2t_ref[...], up_grad).astype(BF)
        grads_ref[2, :, at] = mul(cott_ref[...], activated).astype(BF)
        return carry

    lax.fori_loop(0, hidden // tile, chunk, 0)


def other_mlp_kernel(
    where_ref,
    h2_ref,
    cot_ref,
    first_ref,
    second_ref,
    back_in_ref,
    delta_in_ref,
    resid_ref,
    gain_ref,
    other_gain_ref,
    o_ref,
    out_ref,
    mid_ref,
    mid_bf_ref,
    grad_out_ref,
    w_ref,
    act_ref,
    back_ref,
    delta_ref,
):
    ctx, wt = where_ref[0], where_ref[1]
    rows = h2_ref.shape[0]
    seq = where_ref[2]
    part_width, tok_rows = out_ref.shape
    last = 2 * rows // tok_rows - 1
    half = first_ref.shape[1]
    w_ref[:, pl.ds(pl.multiple_of(seq * half, 16), half), :] = first_ref[...]
    w_ref[:, pl.ds(pl.multiple_of((1 - seq) * half, 16), half), :] = second_ref[...]
    tile = HIDDEN_TILE
    back_ref[...] = back_in_ref[...]
    delta_ref[...] = delta_in_ref[...]

    def chunk(j, carry):
        at = pl.ds(pl.multiple_of(j * tile, tile), tile)
        down = w_ref[2, :, at]
        activated, _, _, back = mlp_chunk(
            h2_ref[...], cot_ref[...], w_ref[0, :, at], w_ref[1, :, at], down
        )
        back_ref[...] += back
        act_ref[...] = activated
        delta_ref[...] += mul(own_rows(act_ref, ctx, last, tok_rows), down, NT)
        return carry

    lax.fori_loop(0, first_ref.shape[2] // tile, chunk, 0)
    gains = in_order(gain_ref[...], other_gain_ref[...], wt, 1)
    layer_out = own_rows(resid_ref, ctx, last, tok_rows) + delta_ref[...]
    out_ref[...] = my_half(layer_out, wt).T.astype(BF)
    resid = resid_ref[...]
    scale = norm_scale(resid)
    normed = resid * scale
    back = back_ref[...]
    gain_grad = jnp.sum(back * normed, axis=0, keepdims=True)
    scaled = back * gains[1:2]
    mean = jnp.mean(scaled * normed, axis=1, keepdims=True)
    mid = cot_ref[...].astype(F32) + scale * (scaled - normed * mean)
    mid_ref[...] = mid
    mid_bf = mid.astype(BF)
    mid_bf_ref[...] = mid_bf
    mid_t = mid.T
    mine = jnp.where(wt == 0, mid_t[:part_width], mid_t[part_width:]).astype(BF)
    grad_out_ref[:part_width] = mul(mine, o_ref[...], NT).astype(BF)
    grad_out_ref[part_width:] = jnp.broadcast_to(gain_grad, (16, gain_grad.shape[1])).astype(BF)


def backward_kernel(
    weights_ref,
    mid_bf_ref,
    q_ref,
    k_ref,
    v_ref,
    o_ref,
    lse_ref,
    cos_ref,
    sin_ref,
    h1_ref,
    own_ref,
    got_ref,
    proj_ref,
    grad_ref,
    gate_out,
    up_out,
    down_out,
    g_ref,
    dk_ref,
    dv_ref,
    sum_ref,
    sems,
):
    rows = q_ref.shape[1]
    query_width = QUERY_HEADS * HEAD_SIZE
    pair_width = KEY_VALUE_HEADS * HEAD_SIZE
    half_dim = HEAD_SIZE // 2
    copies = []
    for i, out in enumerate((gate_out, up_out, down_out)):
        sum_ref[i] = own_ref[i].astype(F32) + got_ref[i].astype(F32)
        copies.append(pltpu.make_async_copy(sum_ref.at[i], out, sems.at[i]))
    for copy in copies:
        copy.start()
    g_ref[...] = mul(weights_ref[query_width + 2 * pair_width :], mid_bf_ref[...], NT).astype(BF)
    repeat = QUERY_HEADS // KEY_VALUE_HEADS
    tile = min(BACKWARD_TILE, rows)
    causal = lax.broadcasted_iota(jnp.int32, (tile, tile), 0) <= lax.broadcasted_iota(
        jnp.int32, (tile, tile), 1
    )

    def unturn(value, start, stop):
        cosines, sines = cos_ref[:, start:stop], sin_ref[:, start:stop]
        low, high = rotated(value[:half_dim], value[half_dim:], cosines, sines, -1.0)
        return jnp.concatenate([low, high], axis=0).astype(BF)

    def group(g, carry):
        pair_at = pl.ds(pl.multiple_of(g * HEAD_SIZE, HEAD_SIZE), HEAD_SIZE)
        keys_t = k_ref[pair_at, :]
        keys, values = turned(keys_t), turned(v_ref[pair_at, :])
        dk_ref[...] = jnp.zeros_like(dk_ref)
        dv_ref[...] = jnp.zeros_like(dv_ref)
        for r in range(repeat):
            head = g * repeat + r
            head_at = pl.ds(pl.multiple_of(head * HEAD_SIZE, HEAD_SIZE), HEAD_SIZE)
            product = g_ref[head_at, :].astype(F32) * o_ref[head_at, :].astype(F32)
            delta = jnp.sum(product, axis=0, keepdims=True)
            for start in range(0, rows, tile):
                stop = start + tile
                query, grad = q_ref[head_at, start:stop], g_ref[head_at, start:stop]
                lse = lse_ref[head, :, start:stop]
                scores = mul(keys[:stop], query)
                prob_grad = mul(values[:stop], grad)
                probs = jnp.where(causal, jnp.exp(scores[start:] - lse), 0.0)
                if start:
                    probs = jnp.concatenate([jnp.exp(scores[:start] - lse), probs], axis=0)
                score_grad = (probs * (prob_grad - delta[:, start:stop])).astype(BF)
                probs = probs.astype(BF)
                dq = mul(keys_t[:, :stop], score_grad) * 0.125
                proj_ref[head_at, start:stop] = unturn(dq, start, stop)
                dk_ref[:, :stop] += mul(query, score_grad, NT)
                dv_ref[:, :stop] += mul(grad, probs, NT)
        key_at = pl.multiple_of(query_width + g * HEAD_SIZE, HEAD_SIZE)
        proj_ref[pl.ds(key_at, HEAD_SIZE), :] = unturn(dk_ref[...], 0, rows)
        value_at = pl.multiple_of(query_width + pair_width + g * HEAD_SIZE, HEAD_SIZE)
        proj_ref[pl.ds(value_at, HEAD_SIZE), :] = dv_ref[...].astype(BF)
        return carry

    lax.fori_loop(0, KEY_VALUE_HEADS, group, 0)
    grad_ref[...] = mul(h1_ref[...], proj_ref[...], NT).astype(BF)
    for copy in copies:
        copy.wait()


def input_kernel(
    where_ref, proj_ref, weights_ref, x_ref, mid_ref, gain_ref, other_gain_ref, out_ref
):
    ctx, wt = where_ref[0], where_ref[1]
    rows = proj_ref.shape[1]
    part_width, tok_rows = out_ref.shape
    last = 2 * rows // tok_rows - 1
    piece = tok_rows // 4
    at = lax.broadcasted_iota(jnp.int32, (rows, tok_rows), 0)
    u = lax.broadcasted_iota(jnp.int32, (rows, tok_rows), 1)
    j = u // piece
    base = jnp.where(j % 2 == 0, ctx, last - ctx)
    position = base * (2 * piece) + (j // 2) * piece + u % piece
    chosen = jnp.where(at == position, 1.0, 0.0).astype(BF)
    mine = mul(proj_ref[...], chosen).astype(BF)
    grad = mul(mine, weights_ref[: proj_ref.shape[0]], TN)
    gains = in_order(gain_ref[...], other_gain_ref[...], wt, 1)
    x = own_rows(x_ref, ctx, last, tok_rows).astype(F32)
    mid = own_rows(mid_ref, ctx, last, tok_rows)
    scale = norm_scale(x)
    normed = x * scale
    scaled = grad * gains[0:1]
    mean = jnp.mean(scaled * normed, axis=1, keepdims=True)
    out_ref[...] = my_half(mid + scale * (scaled - normed * mean), wt).T


def whole_device(layer_input, cotangent, w_qkv, w_out, w_gate, w_up, w_down, gain_attn, gain_mlp):
    ctx_count = lax.axis_size("ctx")
    ctx_index = lax.axis_index("ctx")
    wt_index = lax.axis_index("wt")
    seq_index = lax.axis_index("seq")
    where = jnp.stack([ctx_index, wt_index, seq_index]).astype(jnp.int32)
    tok_rows, part_width = layer_input.shape[1:]
    full_width = 2 * part_width
    rows = tok_rows * ctx_count
    query_width = QUERY_HEADS * HEAD_SIZE
    pair_width = KEY_VALUE_HEADS * HEAD_SIZE
    proj_width = query_width + 2 * pair_width
    hidden = w_gate.shape[1]
    shape = jax.ShapeDtypeStruct

    def across_ctx(value, distance):
        return swap(value, "ctx", distance, ctx_count)

    def half_of(value, axis):
        half = value.shape[axis] // 2
        return lax.dynamic_slice_in_dim(value, seq_index * half, half, axis)

    gains = jnp.stack([gain_attn, gain_mlp])
    block = layer_input[0].T
    one = jnp.stack([block, across_ctx(block, 4)])
    two = across_ctx(one, 2)
    near_one, across_one = across_ctx(one, 1), swap(one, "wt", 1, 2)
    near_two, across_two = across_ctx(two, 1), swap(two, "wt", 1, 2)
    low = swap(near_one, "wt", 1, 2)
    high = across_ctx(across_two, 1)

    other_gains = swap(gains, "wt", 1, 2)
    first = swap(half_of(w_qkv, 0), "wt", 1, 2)
    second = swap(first, "seq", 1, 2)
    out_first = swap(half_of(w_out.T, 0), "wt", 1, 2)
    out_second = swap(out_first, "seq", 1, 2)

    cot = cotangent[0].T
    cot = jnp.stack([cot, swap(cot, "wt", 1, 2)])[None]
    for distance in (1, 2):
        cot = jnp.concatenate([cot, across_ctx(cot, distance)], axis=0)
    cot_far = across_ctx(cot, 4)

    down_t = w_down.T
    mlp_half = jnp.stack([half_of(w_gate, 0), half_of(w_up, 0), half_of(down_t, 0)])
    mlp_half, low, high = lax.optimization_barrier((mlp_half, low, high))
    mlp_first = swap(mlp_half, "wt", 1, 2)
    mlp_second = swap(mlp_first, "seq", 1, 2)

    half_dim = HEAD_SIZE // 2
    frequency = jnp.power(F32(ROPE_BASE), -jnp.arange(half_dim, dtype=F32) * 2.0 / HEAD_SIZE)
    angles = frequency[:, None] * jnp.arange(rows, dtype=F32)[None, :]
    cosines, sines = jnp.cos(angles), jnp.sin(angles)

    x, h1_t, q_t, k_t, v_t, o_t, lse, resid, h2, h2_t, weights = pl.pallas_call(
        forward_kernel,
        in_specs=[SMEM] + [VMEM] * 18,
        out_specs=[VMEM] * 11,
        out_shape=[
            shape((rows, full_width), BF),
            shape((part_width, rows), BF),
            shape((query_width, rows), BF),
            shape((pair_width, rows), BF),
            shape((pair_width, rows), BF),
            shape((query_width, rows), BF),
            shape((QUERY_HEADS, 1, rows), F32),
            shape((rows, full_width), F32),
            shape((rows, full_width), BF),
            shape((full_width, rows), BF),
            shape((proj_width + query_width, full_width), BF),
        ],
        scratch_shapes=[
            pltpu.VMEM((full_width, rows), BF),
            pltpu.VMEM((full_width, proj_width), BF),
            pltpu.VMEM((full_width, query_width), BF),
        ],
        name="forward",
    )(
        where, one, two, near_one, near_two, across_one, across_two, low, high,
        w_qkv, first, second, w_out.T, out_first, out_second,
        gains, other_gains, cosines, sines,
    )

    cots, grads, back, delta = pl.pallas_call(
        own_mlp_kernel,
        in_specs=[SMEM] + [VMEM] * 7,
        out_specs=[VMEM] * 4,
        out_shape=[
            shape((rows, full_width), BF),
            shape((3, full_width, hidden), BF),
            shape((rows, full_width), F32),
            shape((tok_rows, full_width), F32),
        ],
        scratch_shapes=[
            pltpu.VMEM((rows, HIDDEN_TILE), BF),
            pltpu.VMEM((full_width, rows), BF),
        ],
        name="own_mlp",
    )(where, cot, cot_far, h2, h2_t, w_gate, w_up, down_t)
    got = swap(grads, "seq", 1, 2)

    layer_out, mid, mid_bf, grad_out = pl.pallas_call(
        other_mlp_kernel,
        in_specs=[SMEM] + [VMEM] * 10,
        out_specs=[VMEM] * 4,
        out_shape=[
            shape((part_width, tok_rows), BF),
            shape((rows, full_width), F32),
            shape((rows, full_width), BF),
            shape((part_width + 16, query_width), BF),
        ],
        scratch_shapes=[
            pltpu.VMEM((3, full_width, hidden), BF),
            pltpu.VMEM((rows, HIDDEN_TILE), BF),
            pltpu.VMEM((rows, full_width), F32),
            pltpu.VMEM((tok_rows, full_width), F32),
        ],
        name="other_mlp",
    )(where, h2, cots, mlp_first, mlp_second, back, delta, resid, gains, other_gains, o_t)
    got_out = swap(grad_out, "seq", 1, 2)

    proj_t, grad_qkv, grad_gate, grad_up, grad_down_t = pl.pallas_call(
        backward_kernel,
        in_specs=[VMEM] * 12,
        out_specs=[VMEM] * 2 + [ANY] * 3,
        out_shape=[
            shape((proj_width, rows), BF),
            shape((part_width, proj_width), BF),
            shape((full_width, hidden), F32),
            shape((full_width, hidden), F32),
            shape((full_width, hidden), F32),
        ],
        scratch_shapes=[
            pltpu.VMEM((query_width, rows), BF),
            pltpu.VMEM((HEAD_SIZE, rows), F32),
            pltpu.VMEM((HEAD_SIZE, rows), F32),
            pltpu.VMEM((3, full_width, hidden), F32),
            pltpu.SemaphoreType.DMA((3,)),
        ],
        name="backward",
    )(
        weights, mid_bf, q_t, k_t, v_t, o_t, lse, cosines, sines, h1_t,
        grads, got,
    )
    got_qkv = swap(grad_qkv, "seq", 1, 2)
    input_grad = pl.pallas_call(
        input_kernel,
        in_specs=[SMEM] + [VMEM] * 6,
        out_specs=VMEM,
        out_shape=shape((part_width, tok_rows), F32),
        name="input_grad",
    )(where, proj_t, weights, x, mid, gains, other_gains)

    out_sum = grad_out.astype(F32) + got_out.astype(F32)
    qkv_sum = grad_qkv.astype(F32) + got_qkv.astype(F32)
    grad_gain_attn = jnp.sum(qkv_sum * w_qkv.astype(F32), axis=1) / gain_attn
    grad_gain_mlp = lax.dynamic_slice_in_dim(out_sum[part_width], wt_index * part_width, part_width)
    return (
        layer_out.T[None],
        input_grad.T[None],
        qkv_sum,
        out_sum[:part_width].T,
        grad_gate,
        grad_up,
        grad_down_t.T,
        grad_gain_attn,
        grad_gain_mlp,
    )


def solution(mesh):
    in_specs = (
        P("seq", "ctx", "wt"),
        P("seq", "ctx", "wt"),
        P("wt", None),
        P(None, "wt"),
        P(None, "wt"),
        P(None, "wt"),
        P("wt", None),
        P("wt"),
        P("wt"),
    )
    out_specs = (
        P("seq", "ctx", "wt"),
        P("seq", "ctx", "wt"),
        P("wt", None),
        P(None, "wt"),
        P(None, "wt"),
        P(None, "wt"),
        P("wt", None),
        P("wt"),
        P("wt"),
    )
    sizes = mesh.shape
    whole = sizes["wt"] == 2 and sizes["seq"] == 2 and sizes["ctx"] == 8
    return jax.shard_map(
        whole_device if whole else split_device, mesh=mesh, in_specs=in_specs, out_specs=out_specs, check_vma=False
    )
```
